256 devices in a mesh: slab: 32 (over x, z_hi, y), head: 8 (over z_lo, core).
Axes of the slice: x: 4, y: 4, z: 8 (z_hi: 2, z_lo: 4; z = z_hi * 4 + z_lo), core: 2. Of those that a mesh axis runs over, the one named last changes fastest.
Arguments:
- inputs: bfloat16 [32768, 1024], P('slab'), may hold values from -6 to 6
- norm_gain: float32 [1024], replicated, may hold values from 0.1 to 1.9
- query_weight: bfloat16 [1024, 1024], P('slab', 'head'), may hold values from -0.1875 to 0.1875
- key_weight: bfloat16 [1024, 1024], P('slab', 'head'), may hold values from -0.1875 to 0.1875
- value_weight: bfloat16 [1024, 1024], P('slab', 'head'), may hold values from -0.1875 to 0.1875
- out_weight: bfloat16 [1024, 1024], P('head', 'slab'), may hold values from -0.1875 to 0.1875
- logit_scale: float32 [16], P('head'), may hold values from 0.5 to 4, as said below
- grad_output: bfloat16 [32768, 1024], P('slab'), may hold values from -6 to 6
Outputs:
- grad_inputs: bfloat16 [32768, 1024], P('slab', 'head')
- grad_gain: float32 [1024], P('head')
- grad_query_weight: float32 [1024, 1024], P('slab', 'head')
- grad_key_weight: float32 [1024, 1024], P('slab', 'head')
- grad_value_weight: float32 [1024, 1024], P('slab', 'head')
- grad_out_weight: float32 [1024, 1024], P('head', 'slab')
The draws below stay inside these ranges and needn't reach their ends.
Inputs may be any that keep to these rules, and one draw needn't show every extreme that they name: `logit_scale`: positive multipliers of each head's attention logits.
All inputs are finite; a program needn't handle non-finite values.
Results may differ from the reference program's by a relative error of at most 0.015.
The reference program's roundings to bfloat16 on the way count: a program that leaves them out, or rounds other values in their place, can miss the bound.
Values may be sent and summed in bfloat16 or wider, within the bound.
No kernel may reach another device: no remote copies, remote signals or barrier semaphores. Data moves between devices by JAX's collectives and lax.ppermute only.
A program may use at most 128 MiB of HBM per device.

```python
import math
import jax
import jax.numpy as jnp
from jax import lax

D = 1024
H = 16
HD = 64
NX = 32
NY = 32
NZ = 32
TOKENS = 32768
N_HEAD = 8


def draw_logit_scale(key, part):
    gentle = jnp.exp(jax.random.uniform(key, (H,), jnp.float32, math.log(0.5), math.log(2.0)))
    mixed = gentle
    picked = jax.random.randint(jax.random.fold_in(key, 7), (), 0, H)
    return jnp.where(jnp.arange(H) == picked, 4.0, mixed).astype(jnp.float32)


def level_of(rng, shape, shards, smallest, top_value):
    gain, own = 1.0, jax.random.fold_in(rng, 6)
    for axis_at, blocks in shards:
        steps = jnp.exp(jax.random.uniform(jax.random.fold_in(own, axis_at), (blocks,), jnp.float32, smallest / len(shards), top_value / len(shards)))
        gain = gain * jnp.repeat(steps, shape[axis_at] // blocks).reshape([-1 if axis == axis_at else 1 for axis in range(len(shape))])
    return gain


def normal_values(stream_key, extent, width, reach, shards=(), kind=jnp.bfloat16):
    entries = jax.random.normal(stream_key, extent, jnp.float32) * width
    if len(shards) > 0:
        entries = level_of(stream_key, extent, shards, -0.22, 0.18) * entries
    return jnp.clip(entries, min=-reach, max=reach).astype(kind)


def setup_inputs(seed: int = 0) -> dict:
    key_of = jax.random.split(jax.random.key(seed), 9)
    inputs = normal_values(key_of[0], (TOKENS, D), 1.0, 6.0, ((0, 32),))
    norm_gain = jnp.clip(1.0 + 0.18 * jax.random.normal(key_of[1], (D,), jnp.float32), 0.1, 1.9)
    query_weight = normal_values(key_of[2], (D, D), D ** -0.5, 0.1875, ((0, 32), (1, 8)))
    key_weight = normal_values(key_of[3], (D, D), D ** -0.5, 0.1875, ((0, 32), (1, 8)))
    value_weight = normal_values(key_of[4], (D, D), D ** -0.5, 0.1875, ((0, 32), (1, 8)))
    out_weight = normal_values(key_of[5], (D, D), D ** -0.5, 0.1875, ((0, 8), (1, 32)))
    logit_scale = draw_logit_scale(jax.random.fold_in(key_of[8], 71), 0)
    grad_output = normal_values(key_of[7], (TOKENS, D), 1.0, 6.0, ((0, 32),))
    return {"inputs": inputs, "norm_gain": norm_gain, "query_weight": query_weight, "key_weight": key_weight, "value_weight": value_weight, "out_weight": out_weight, "logit_scale": logit_scale, "grad_output": grad_output}


def line_reference(queries, key_rows, values, grad_attn, scale_factor):
    query_float = queries.astype(jnp.float32)
    key_float = key_rows.astype(jnp.float32)
    value_float = values.astype(jnp.float32)
    gradient_float = grad_attn.astype(jnp.float32)
    score_matrix = jnp.einsum('iwo,ico->iwc', query_float, key_float) * scale_factor
    highest = lax.optimization_barrier(jnp.max(score_matrix, axis=-1, keepdims=True))
    exponent = jnp.exp(score_matrix - highest)
    softmax_p = exponent / lax.optimization_barrier(jnp.sum(exponent, axis=-1, keepdims=True))
    rounded_probability = softmax_p.astype(jnp.bfloat16).astype(jnp.float32)
    output_rows = jnp.einsum('czi,civ->czv', rounded_probability, value_float)
    probability_gradient = jnp.einsum('iwo,ico->iwc', gradient_float, value_float)
    row_delta = lax.optimization_barrier(jnp.sum(gradient_float * output_rows, axis=-1))
    score_gradient = (softmax_p * (probability_gradient - row_delta[..., None]) * scale_factor).astype(jnp.bfloat16).astype(jnp.float32)
    query_gradient = jnp.einsum('czi,civ->czv', score_gradient, key_float)
    key_gradient = jnp.einsum('jeu,jet->jut', score_gradient, query_float)
    value_gradient = jnp.einsum('jeu,jet->jut', rounded_probability, gradient_float)
    return (output_rows, query_gradient, key_gradient, value_gradient)

def along_lines(grids, scale_factor):
    moved = tuple((jnp.transpose(grid, (2, 0, 1, 3)) for grid in grids))

    def one_head(operands):
        return line_reference(operands[0], operands[1], operands[2], operands[3], operands[4])
    results = lax.map(one_head, moved + (scale_factor,))
    return tuple((jnp.transpose(result, (1, 2, 0, 3)) for result in results))

def reference(inputs, norm_gain, query_weight, key_weight, value_weight, out_weight, logit_scale, grad_output):
    features = inputs.astype(jnp.float32)
    inv_rms = lax.rsqrt(lax.optimization_barrier(jnp.mean(features * features, axis=1)) + 1e-06)
    normed = (features * inv_rms[:, None] * norm_gain[None, :]).astype(jnp.bfloat16)
    queries = jnp.dot(normed, query_weight, preferred_element_type=jnp.float32).astype(jnp.bfloat16)
    key_rows = jnp.dot(normed, key_weight, preferred_element_type=jnp.float32).astype(jnp.bfloat16)
    values = jnp.dot(normed, value_weight, preferred_element_type=jnp.float32).astype(jnp.bfloat16)
    grad_attn = jnp.dot(grad_output, out_weight.T, preferred_element_type=jnp.float32).astype(jnp.bfloat16)
    scale_factor = logit_scale / math.sqrt(HD)
    grids = tuple((array.reshape(NZ, NY, NX, H, HD) for array in (queries, key_rows, values, grad_attn)))
    along_x = along_lines(tuple((grid.reshape(NZ * NY, NX, H, HD) for grid in grids)), scale_factor)
    along_x = tuple((result.reshape(NZ, NY, NX, H, HD) for result in along_x))
    along_y = along_lines(tuple((jnp.transpose(grid, (0, 2, 1, 3, 4)).reshape(NZ * NX, NY, H, HD) for grid in grids)), scale_factor)
    along_y = tuple((jnp.transpose(result.reshape(NZ, NX, NY, H, HD), (0, 2, 1, 3, 4)) for result in along_y))
    along_z = along_lines(tuple((jnp.transpose(grid, (1, 2, 0, 3, 4)).reshape(NY * NX, NZ, H, HD) for grid in grids)), scale_factor)
    along_z = tuple((jnp.transpose(result.reshape(NY, NX, NZ, H, HD), (2, 0, 1, 3, 4)).astype(jnp.bfloat16) for result in along_z))
    combined = tuple(((along_x[index] + along_y[index] + along_z[index].astype(jnp.float32)).astype(jnp.bfloat16).reshape(TOKENS, D) for index in range(4)))
    attn, query_gradient, key_gradient, value_gradient = combined
    share = D // N_HEAD
    grad_normed = jnp.zeros((TOKENS, D), jnp.float32)
    for group_index in range(N_HEAD):
        low = group_index * share
        partial_sum = jnp.dot(query_gradient[:, low:low + share], query_weight[:, low:low + share].T, preferred_element_type=jnp.float32)
        partial_sum = partial_sum + jnp.dot(key_gradient[:, low:low + share], key_weight[:, low:low + share].T, preferred_element_type=jnp.float32)
        partial_sum = partial_sum + jnp.dot(value_gradient[:, low:low + share], value_weight[:, low:low + share].T, preferred_element_type=jnp.float32)
        grad_normed = grad_normed + partial_sum.astype(jnp.bfloat16).astype(jnp.float32)
    row_dot = lax.optimization_barrier(jnp.sum(norm_gain[None, :] * grad_normed * features, axis=1))
    grad_inputs = (inv_rms[:, None] * norm_gain[None, :] * grad_normed - features * (inv_rms ** 3)[:, None] * row_dot[:, None] / D).astype(jnp.bfloat16)
    loss_scale = 1.0 / math.sqrt(TOKENS)
    grad_gain = lax.optimization_barrier(jnp.sum(grad_normed * features * inv_rms[:, None], axis=0)) * loss_scale
    grad_query_weight = jnp.dot(normed.T, query_gradient, preferred_element_type=jnp.float32) * loss_scale
    grad_key_weight = jnp.dot(normed.T, key_gradient, preferred_element_type=jnp.float32) * loss_scale
    grad_value_weight = jnp.dot(normed.T, value_gradient, preferred_element_type=jnp.float32) * loss_scale
    grad_out_weight = jnp.dot(attn.T, grad_output, preferred_element_type=jnp.float32) * loss_scale
    return (grad_inputs, grad_gain, grad_query_weight, grad_key_weight, grad_value_weight, grad_out_weight)
```

```python
import functools
import math

import jax
import jax.numpy as jnp
from jax import lax
from jax.experimental import pallas as pl
from jax.experimental.pallas import tpu as pltpu
from jax.sharding import PartitionSpec as P

BF = jnp.bfloat16
F32 = jnp.float32
SIDE = 32
LANES = 128
TOK = SIDE * SIDE
NEG = -1e30
VM = 40 << 20


def dot(a, b, ca, cb):
    return lax.dot_general(a, b, (((ca,), (cb,)), ((), ())), preferred_element_type=F32)


def call(body, outs, name, **kw):
    return pl.pallas_call(
        body,
        out_shape=outs,
        name=name,
        compiler_params=pltpu.CompilerParams(vmem_limit_bytes=VM),
        **kw,
    )


def shape(dims, kind):
    return jax.ShapeDtypeStruct(dims, kind)


def spread_body(q_ref, k_ref, v_ref, o_ref, out_ref):
    for j, ref in enumerate((q_ref, k_ref, v_ref)):
        out_ref[:, :, j * LANES : (j + 1) * LANES] = jnp.broadcast_to(
            ref[...][None], (SIDE, SIDE, LANES)
        )
    turned = o_ref[...].astype(F32).T.astype(BF)
    out_ref[:, :, 3 * LANES :] = jnp.broadcast_to(turned[None], (SIDE, SIDE, LANES))


def project_body(x_ref, go_ref, gain_ref, w_ref, out_ref, normed_ref, inv_ref):
    x = x_ref[...].astype(F32)
    rows, width = x.shape
    inv = lax.rsqrt(jnp.sum(x * x, axis=1, keepdims=True) / width + 1e-06)
    normed = (x * inv * gain_ref[...]).astype(BF)
    normed_ref[...] = normed
    inv_ref[...] = jnp.broadcast_to(inv, inv_ref.shape)
    three = dot(normed, w_ref[:, : 3 * LANES], 1, 0)
    last = dot(go_ref[...], w_ref[:, 3 * LANES :], 1, 0)
    for j in range(4):
        part = three[:, j * LANES : (j + 1) * LANES] if j < 3 else last
        out_ref[:, j] = part.astype(BF).reshape(rows // SIDE, SIDE, LANES)


def first_head(rows):
    return lax.broadcasted_iota(jnp.int32, (rows, LANES), 1) < LANES // 2


def stacked(a):
    rows = a.shape[0]
    keep = first_head(rows)
    zero = jnp.zeros_like(a)
    return jnp.concatenate([jnp.where(keep, a, zero), jnp.where(keep, zero, a)], axis=0)


def folded(a):
    rows = a.shape[0] // 2
    return jnp.where(first_head(rows), a[:rows], a[rows:])


def attend(q, k, v, g, factors, bias):
    rows = q.shape[0]
    k2, v2 = stacked(k), stacked(v)
    s = dot(q, k2, 1, 1)
    dp = dot(g, v2, 1, 1)
    probs = []
    for h in range(2):
        sh = s[:, h * rows : (h + 1) * rows] * factors[h] + bias
        top = jnp.max(sh, axis=1, keepdims=True)
        e = jnp.exp(sh - top)
        probs.append(e / jnp.sum(e, axis=1, keepdims=True))
    pb = jnp.concatenate([p.astype(BF) for p in probs], axis=1)
    out = dot(pb, v2, 1, 0)
    go = g.astype(F32) * out
    keep = first_head(rows)
    grads = []
    for h in range(2):
        mine = jnp.where(keep, go, 0.0) if h == 0 else jnp.where(keep, 0.0, go)
        delta = jnp.sum(mine, axis=1, keepdims=True)
        dh = dp[:, h * rows : (h + 1) * rows]
        grads.append((probs[h] * (dh - delta) * factors[h]).astype(BF))
    ds = jnp.concatenate(grads, axis=1)
    gq = dot(ds, k2, 1, 0)
    gk = folded(dot(ds, q, 0, 0))
    gv = folded(dot(pb, g, 0, 0))
    return out, gq, gk, gv


def same_line(rows, line):
    a = line(lax.broadcasted_iota(jnp.int32, (rows, rows), 0))
    b = line(lax.broadcasted_iota(jnp.int32, (rows, rows), 1))
    return jnp.where(a == b, 0.0, NEG).astype(F32)


def strided_lines(in_ref, f_ref, wide_ref, bias_ref, add):
    for j in range(4):
        wide_ref[j] = in_ref[:, j].astype(F32).reshape(SIDE, 4, 8, LANES)
    rows = 8 * SIDE
    bias_ref[...] = same_line(rows, lambda i: i % 8)
    factors = (f_ref[0], f_ref[1])

    def step(b, _):
        parts = [wide_ref[j, :, b].reshape(rows, LANES).astype(BF) for j in range(4)]
        for j, r in enumerate(attend(*parts, factors, bias_ref[...])):
            add(j, b, r.reshape(SIDE, 8, LANES))
        return 0

    lax.fori_loop(0, 4, step, 0)


def plane_body(in_ref, f_ref, out_ref, wide_ref, bias_ref, bias_x_ref):
    rows = 4 * SIDE
    bias_x_ref[...] = same_line(rows, lambda i: i // SIDE)
    factors = (f_ref[0], f_ref[1])

    def step(b, _):
        parts = [in_ref[pl.ds(4 * b, 4), j].reshape(rows, LANES) for j in range(4)]
        for j, r in enumerate(attend(*parts, factors, bias_x_ref[...])):
            out_ref[j, pl.ds(4 * b, 4)] = r.reshape(4, 4, 8, LANES)
        return 0

    lax.fori_loop(0, 8, step, 0)

    def add(j, b, r):
        out_ref[j, :, b] += r

    strided_lines(in_ref, f_ref, wide_ref, bias_ref, add)


def depth_body(in_ref, f_ref, out_ref, wide_ref, res_ref, bias_ref):
    def add(j, b, r):
        res_ref[j, :, b] = r

    strided_lines(in_ref, f_ref, wide_ref, bias_ref, add)
    for j in range(4):
        out_ref[:, j] = res_ref[j].reshape(SIDE, SIDE, LANES).astype(BF)


def halves(a):
    high = a.astype(BF)
    return high, (a - high.astype(F32)).astype(BF)


def combine_body(
    h_ref, loc_ref, back_ref, proj_ref, normed_ref, go_ref, w_ref,
    away_ref, keep_ref, dots_ref, wg_ref, g_ref,
):
    zl, core = h_ref[0] // 2, h_ref[0] % 2
    total = jnp.zeros((TOK, LANES), F32)
    for j in range(4):
        part = loc_ref[j].reshape(TOK, LANES) + back_ref[:, j].astype(F32).reshape(TOK, LANES)
        part = part.astype(BF)
        at = (j - 1) % 4
        g_ref[:, at * LANES : (at + 1) * LANES] = part
        if j > 0:
            total += part.astype(F32) * proj_ref[:, j - 1].astype(F32).reshape(TOK, LANES)
    rows = [
        jnp.sum(total[i * LANES : (i + 1) * LANES].T, axis=0, keepdims=True) for i in range(8)
    ]
    dots = jnp.concatenate(rows, axis=0)
    dots_ref[...] = dots
    high, low = halves(dots)
    away_ref[4 * TOK : 4 * TOK + 8] = high
    away_ref[4 * TOK + 8 :] = low

    def block(h):
        w = w_ref[pl.ds(pl.multiple_of(h * LANES, LANES), LANES), : 3 * LANES]
        return dot(g_ref[:, : 3 * LANES], w, 1, 1).astype(BF)

    def step(i, _):
        away_ref[pl.ds(pl.multiple_of(i * TOK, TOK), TOK)] = block(2 * i + 1 - core)
        keep_ref[i] = block(2 * i + core)
        return 0

    lax.fori_loop(0, 4, step, 0)

    def wstep(i, _):
        at = pl.ds(pl.multiple_of(i * 256, 256), 256)
        three = dot(normed_ref[:, at], g_ref[:, : 3 * LANES], 0, 0)
        last = dot(go_ref[:, at], g_ref[:, 3 * LANES :], 0, 0)
        for j in range(4):
            part = three[:, j * LANES : (j + 1) * LANES] if j < 3 else last
            wg_ref[pl.ds(8 * i, 8), j] = part.astype(BF).reshape(8, SIDE, LANES)
        return 0

    lax.fori_loop(0, 4, wstep, 0)


def pair_body(h_ref, got_ref, keep_ref, dots_ref, s1_ref, s2_ref, s3_ref, own_ref, both_ref):
    zl = h_ref[0] // 2
    dots = dots_ref[...] + got_ref[4 * TOK : 4 * TOK + 8].astype(F32)
    dots = dots + got_ref[4 * TOK + 8 :].astype(F32)
    both_ref[...] = dots
    high, low = halves(dots)

    def block(i):
        mine = keep_ref[i].astype(F32)
        return mine + got_ref[pl.ds(pl.multiple_of(i * TOK, TOK), TOK)].astype(F32)

    for d, ref in enumerate((s1_ref, s2_ref, s3_ref)):
        ref[:TOK] = block((zl + d + 1) % 4).astype(BF)
        ref[TOK : TOK + 8] = high
        ref[TOK + 8 :] = low
    own_ref[...] = block(zl)


def norm_body(
    h_ref, x_ref, gain_ref, own_ref, r1_ref, r2_ref, r3_ref, dots_ref, inv_ref, gx_ref, tail_ref
):
    grad = own_ref[...]
    dots = dots_ref[...]
    for ref in (r1_ref, r2_ref, r3_ref):
        grad = grad + ref[:TOK].astype(F32)
        dots = dots + ref[TOK : TOK + 8].astype(F32) + ref[TOK + 8 :].astype(F32)
    cols = [
        jnp.broadcast_to(dots[i : i + 1], (LANES, LANES)).T for i in range(8)
    ]
    row_dot = jnp.concatenate(cols, axis=0)
    x = x_ref[...].astype(F32)
    inv = inv_ref[...]
    gx = inv * gain_ref[...] * grad - x * (inv * inv) * row_dot * (1.0 / 1024)
    gx_ref[...] = gx.astype(BF)
    gain = jnp.sum(grad * x * inv, axis=0, keepdims=True)
    high, low = halves(gain)
    first = lax.broadcasted_iota(jnp.int32, (8, LANES), 0) == 0
    zero = jnp.zeros((8, LANES), F32)
    tail_ref[...] = jnp.concatenate(
        [
            jnp.where(first, jnp.broadcast_to(high.astype(F32), (8, LANES)), zero),
            jnp.where(first, jnp.broadcast_to(low.astype(F32), (8, LANES)), zero),
        ],
        axis=0,
    ).astype(BF)


def sum_body(in_ref, q_ref, k_ref, v_ref, o_ref, gain_ref, *, scale):
    acc = in_ref[0].astype(F32)
    for i in range(1, SIDE):
        acc = acc + in_ref[i].astype(F32)
    acc = acc * scale
    for j, ref in enumerate((q_ref, k_ref, v_ref)):
        ref[...] = acc[j * SIDE : (j + 1) * SIDE]
    o_ref[...] = acc[3 * SIDE : 4 * SIDE].T
    gain_ref[...] = acc[4 * SIDE : 4 * SIDE + 1] + acc[4 * SIDE + 8 : 4 * SIDE + 9]


SMEM = pl.BlockSpec(memory_space=pltpu.SMEM)
VMEM = pl.BlockSpec(memory_space=pltpu.VMEM)


def body(
    inputs, norm_gain, query_weight, key_weight, value_weight, out_weight, logit_scale, grad_output
):
    rows, width = inputs.shape
    head_dim = 64
    head = lax.axis_index("head").astype(jnp.int32).reshape(1)
    gain = norm_gain.reshape(1, width)
    factors = logit_scale / math.sqrt(head_dim)

    spread = call(spread_body, shape((SIDE, SIDE, 4 * LANES), BF), "spread")(
        query_weight, key_weight, value_weight, out_weight
    )
    weights = lax.all_to_all(spread, "slab", 0, 0, tiled=True).reshape(width, 4 * LANES)

    blk = 256
    proj, normed, inv = call(
        project_body,
        (
            shape((SIDE, 4, SIDE, LANES), BF),
            shape((rows, width), BF),
            shape((rows, LANES), F32),
        ),
        "project",
        grid=(rows // blk,),
        in_specs=[
            pl.BlockSpec((blk, width), lambda i: (i, 0)),
            pl.BlockSpec((blk, width), lambda i: (i, 0)),
            pl.BlockSpec((1, width), lambda i: (0, 0)),
            pl.BlockSpec((width, 4 * LANES), lambda i: (0, 0)),
        ],
        out_specs=(
            pl.BlockSpec((blk // SIDE, 4, SIDE, LANES), lambda i: (i, 0, 0, 0)),
            pl.BlockSpec((blk, width), lambda i: (i, 0)),
            pl.BlockSpec((blk, LANES), lambda i: (i, 0)),
        ),
    )(inputs, grad_output, gain, weights)

    moved = lax.all_to_all(proj, "slab", 0, 0, tiled=True)
    big = (4, SIDE, 4, 8, LANES)
    local = call(
        plane_body,
        shape(big, F32),
        "plane",
        in_specs=[VMEM, SMEM],
        scratch_shapes=[
            pltpu.VMEM(big, F32),
            pltpu.VMEM((256, 256), F32),
            pltpu.VMEM((128, 128), F32),
        ],
    )(proj, factors)
    z_terms = call(
        depth_body,
        shape((SIDE, 4, SIDE, LANES), BF),
        "depth",
        in_specs=[VMEM, SMEM],
        scratch_shapes=[
            pltpu.VMEM(big, F32),
            pltpu.VMEM(big, F32),
            pltpu.VMEM((256, 256), F32),
        ],
    )(moved, factors)
    back = lax.all_to_all(z_terms, "slab", 0, 0, tiled=True)

    away, keep, dots, wg = call(
        combine_body,
        (
            shape((4 * TOK + 16, LANES), BF),
            shape((4, TOK, LANES), BF),
            shape((8, LANES), F32),
            shape((SIDE, 4, SIDE, LANES), BF),
        ),
        "combine",
        in_specs=[SMEM] + [VMEM] * 6,
        scratch_shapes=[pltpu.VMEM((TOK, 4 * LANES), BF)],
    )(head, local, back, proj, normed, grad_output, weights)

    got = lax.ppermute(away, "head", [(i, i ^ 1) for i in range(8)])
    piece = shape((TOK + 16, LANES), BF)
    s1, s2, s3, own, dots = call(
        pair_body,
        (piece, piece, piece, shape((TOK, LANES), F32), shape((8, LANES), F32)),
        "pair",
        in_specs=[SMEM] + [VMEM] * 3,
    )(head, got, keep, dots)
    r1, r2, r3 = (
        lax.ppermute(s, "head", [(i, (i + 2 * d) % 8) for i in range(8)])
        for d, s in ((1, s1), (2, s2), (3, s3))
    )

    whole = lambda dims: pl.BlockSpec(dims, lambda i, h: (0,) * len(dims))
    grad_inputs, tail = pl.pallas_call(
        norm_body,
        out_shape=(shape((rows, LANES), BF), shape((16, LANES), BF)),
        name="norm_back",
        grid_spec=pltpu.PrefetchScalarGridSpec(
            num_scalar_prefetch=1,
            grid=(1,),
            in_specs=[
                pl.BlockSpec((rows, LANES), lambda i, h: (0, h[0])),
                pl.BlockSpec((1, LANES), lambda i, h: (0, h[0])),
                whole((TOK, LANES)),
                whole((TOK + 16, LANES)),
                whole((TOK + 16, LANES)),
                whole((TOK + 16, LANES)),
                whole((8, LANES)),
                whole((TOK, LANES)),
            ],
            out_specs=(whole((rows, LANES)), whole((16, LANES))),
        ),
        compiler_params=pltpu.CompilerParams(vmem_limit_bytes=VM),
    )(head, inputs, gain, own, r1, r2, r3, dots, inv)

    sent = jnp.concatenate(
        [wg.reshape(SIDE, 4 * SIDE, LANES), jnp.broadcast_to(tail[None], (SIDE, 16, LANES))],
        axis=1,
    )
    pieces = lax.all_to_all(sent, "slab", 0, 0, tiled=True)
    part = shape((SIDE, LANES), F32)
    gqw, gkw, gvw, gow, ggain = call(
        functools.partial(sum_body, scale=1.0 / math.sqrt(rows * SIDE)),
        (part, part, part, shape((LANES, SIDE), F32), shape((1, LANES), F32)),
        "slab_sum",
    )(pieces)
    return grad_inputs, ggain.reshape(LANES), gqw, gkw, gvw, gow


def solution(mesh):
    in_specs = (
        P("slab", None),
        P(),
        P("slab", "head"),
        P("slab", "head"),
        P("slab", "head"),
        P("head", "slab"),
        P("head"),
        P("slab", None),
    )
    out_specs = (
        P("slab", "head"),
        P("head"),
        P("slab", "head"),
        P("slab", "head"),
        P("slab", "head"),
        P("head", "slab"),
    )
    return jax.shard_map(body, mesh=mesh, in_specs=in_specs, out_specs=out_specs, check_vma=False)
```

```python
import functools
import math

import jax
import jax.numpy as jnp
from jax import lax
from jax.experimental import pallas as pl
from jax.experimental.pallas import tpu as pltpu
from jax.sharding import PartitionSpec as P

BF = jnp.bfloat16
F32 = jnp.float32
SIDE = 32
LANES = 128
TOK = SIDE * SIDE
NEG = -1e30
VM = 20 << 20


def dot(a, b, ca, cb):
    return lax.dot_general(a, b, (((ca,), (cb,)), ((), ())), preferred_element_type=F32)


def call(body, outs, name, **kw):
    return pl.pallas_call(
        body,
        out_shape=outs,
        name=name,
        compiler_params=pltpu.CompilerParams(vmem_limit_bytes=VM),
        **kw,
    )


def shape(dims, kind):
    return jax.ShapeDtypeStruct(dims, kind)


def places(at_ref):
    head, slab = at_ref[0], at_ref[1]
    return head // 2, head % 2, slab // 8, (slab // 4) % 2, slab % 4


def rows_at(i, count):
    return pl.ds(pl.multiple_of(i * count, count), count)


def pack_body(q_ref, k_ref, v_ref, o_ref, out_ref, o_buf, part_buf, sems):
    copies = [
        pltpu.make_async_copy(src, part_buf.at[j], sems.at[j])
        for j, src in enumerate((q_ref, k_ref, v_ref))
    ] + [pltpu.make_async_copy(o_ref, o_buf, sems.at[3])]
    for c in copies:
        c.start()
    for c in copies:
        c.wait()
    for j in range(3):
        out_ref[:, j * LANES : (j + 1) * LANES] = part_buf[j]
    out_ref[:, 3 * LANES :] = o_buf[...].astype(F32).T.astype(BF)


def pair_up_body(at_ref, mine_ref, got_ref, one_ref, two_ref):
    _, _, _, zh, _ = places(at_ref)
    for place, ref in ((zh, mine_ref), (1 - zh, got_ref)):
        one_ref[rows_at(place, SIDE)] = ref[:, : 2 * LANES]
        two_ref[rows_at(place, SIDE)] = ref[:, 2 * LANES :]


def line_up_body(at_ref, *refs):
    _, _, x, _, y = places(at_ref)
    for n, place in enumerate((x, y)):
        for d in range(4):
            refs[8 + n][rows_at((place + 4 - d) % 4, 2 * SIDE)] = refs[4 * n + d][...]


def norm_stats_body(x_ref, gain_ref, normed_ref, inv_ref):
    x = x_ref[...].astype(F32)
    width = x.shape[1]
    inv = lax.rsqrt(jnp.sum(x * x, axis=1, keepdims=True) / width + 1e-06)
    normed_ref[...] = (x * inv * gain_ref[...]).astype(BF)
    inv_ref[...] = jnp.broadcast_to(inv, inv_ref.shape)


def project_body(at_ref, normed_ref, go_ref, *refs):
    pieces, out_ref, w_ref = refs[:8], refs[8], refs[9]
    _, _, x, _, y = places(at_ref)
    for d in range(4):
        far_y, far_x = (y + 4 - d) % 4, (x + 4 - d) % 4
        for near in range(4):
            for zh in range(2):
                rows = slice((near * 2 + zh) * SIDE, (near * 2 + zh + 1) * SIDE)
                at = rows_at(near * 8 + zh * 4 + far_y, SIDE)
                w_ref[at, : 2 * LANES] = pieces[d][rows]
                at = rows_at(far_x * 8 + zh * 4 + near, SIDE)
                w_ref[at, 2 * LANES :] = pieces[4 + d][rows]

    def step(i, _):
        at = rows_at(i, 256)
        three = dot(normed_ref[at], w_ref[:, : 3 * LANES], 1, 0)
        last = dot(go_ref[at], w_ref[:, 3 * LANES :], 1, 0)
        for j in range(4):
            part = three[:, j * LANES : (j + 1) * LANES] if j < 3 else last
            out_ref[pl.ds(8 * i, 8), j] = part.astype(BF).reshape(8, SIDE, LANES)
        return 0

    lax.fori_loop(0, 4, step, 0)


def first_head(rows):
    return lax.broadcasted_iota(jnp.int32, (rows, LANES), 1) < LANES // 2


def stacked(a):
    rows = a.shape[0]
    keep = first_head(rows)
    zero = jnp.zeros_like(a)
    return jnp.concatenate([jnp.where(keep, a, zero), jnp.where(keep, zero, a)], axis=0)


def folded(a):
    rows = a.shape[0] // 2
    return jnp.where(first_head(rows), a[:rows], a[rows:])


def attend(q, k, v, g, factors, bias):
    rows = q.shape[0]
    k2, v2 = stacked(k), stacked(v)
    s = dot(q, k2, 1, 1)
    dp = dot(g, v2, 1, 1)
    probs = []
    for h in range(2):
        sh = s[:, h * rows : (h + 1) * rows] * factors[h] + bias
        top = jnp.max(sh, axis=1, keepdims=True)
        e = jnp.exp(sh - top)
        probs.append(e / jnp.sum(e, axis=1, keepdims=True))
    pb = jnp.concatenate([p.astype(BF) for p in probs], axis=1)
    out = dot(pb, v2, 1, 0)
    go = g.astype(F32) * out
    keep = first_head(rows)
    grads = []
    for h in range(2):
        mine = jnp.where(keep, go, 0.0) if h == 0 else jnp.where(keep, 0.0, go)
        delta = jnp.sum(mine, axis=1, keepdims=True)
        dh = dp[:, h * rows : (h + 1) * rows]
        grads.append((probs[h] * (dh - delta) * factors[h]).astype(BF))
    ds = jnp.concatenate(grads, axis=1)
    gq = dot(ds, k2, 1, 0)
    gk = folded(dot(ds, q, 0, 0))
    gv = folded(dot(pb, g, 0, 0))
    return out, gq, gk, gv


def same_line(rows, line):
    a = line(lax.broadcasted_iota(jnp.int32, (rows, rows), 0))
    b = line(lax.broadcasted_iota(jnp.int32, (rows, rows), 1))
    return jnp.where(a == b, 0.0, NEG).astype(F32)


def strided_lines(in_ref, f_ref, wide_ref, bias_ref, add):
    for j in range(4):
        wide_ref[j] = in_ref[:, j].astype(F32).reshape(SIDE, 4, 8, LANES)
    rows = 8 * SIDE
    bias_ref[...] = same_line(rows, lambda i: i % 8)
    factors = (f_ref[0], f_ref[1])

    def step(b, _):
        parts = [wide_ref[j, :, b].reshape(rows, LANES).astype(BF) for j in range(4)]
        for j, r in enumerate(attend(*parts, factors, bias_ref[...])):
            add(j, b, r.reshape(SIDE, 8, LANES))
        return 0

    lax.fori_loop(0, 4, step, 0)


def plane_body(in_ref, f_ref, out_ref, wide_ref, bias_ref, bias_x_ref):
    rows = 4 * SIDE
    bias_x_ref[...] = same_line(rows, lambda i: i // SIDE)
    factors = (f_ref[0], f_ref[1])

    def step(b, _):
        parts = [in_ref[pl.ds(4 * b, 4), j].reshape(rows, LANES) for j in range(4)]
        for j, r in enumerate(attend(*parts, factors, bias_x_ref[...])):
            out_ref[j, pl.ds(4 * b, 4)] = r.reshape(4, 4, 8, LANES)
        return 0

    lax.fori_loop(0, 8, step, 0)

    def add(j, b, r):
        out_ref[j, :, b] += r

    strided_lines(in_ref, f_ref, wide_ref, bias_ref, add)


def depth_body(in_ref, f_ref, out_ref, wide_ref, res_ref, bias_ref):
    def add(j, b, r):
        res_ref[j, :, b] = r

    strided_lines(in_ref, f_ref, wide_ref, bias_ref, add)
    for j in range(4):
        out_ref[:, j] = res_ref[j].reshape(SIDE, SIDE, LANES).astype(BF)


def halves(a):
    high = a.astype(BF)
    return high, (a - high.astype(F32)).astype(BF)


def combine_body(
    at_ref, loc_ref, back_ref, proj_ref, normed_ref, gain_ref, w_ref,
    away_ref, keep_ref, small_ref, g_ref,
):
    _, core, _, _, _ = places(at_ref)
    total = jnp.zeros((TOK, LANES), F32)
    for j in range(4):
        part = loc_ref[j].reshape(TOK, LANES) + back_ref[:, j].astype(F32).reshape(TOK, LANES)
        part = part.astype(BF)
        at = (j - 1) % 4
        g_ref[:, at * LANES : (at + 1) * LANES] = part
        if j > 0:
            total += part.astype(F32) * proj_ref[:, j - 1].astype(F32).reshape(TOK, LANES)
    for i in range(8):
        row = jnp.sum(total[i * LANES : (i + 1) * LANES].T, axis=0, keepdims=True)
        small_ref[i : i + 1] = row

    def block(h):
        w = w_ref[rows_at(h, LANES), : 3 * LANES]
        part = dot(g_ref[:, : 3 * LANES], w, 1, 1).astype(BF)
        n = normed_ref[:, rows_at(h, LANES)].astype(F32)
        gain = jnp.sum(part.astype(F32) * n, axis=0, keepdims=True) / gain_ref[pl.ds(h, 1)]
        return part, gain

    def step(i, _):
        part, gain = block(2 * i + 1 - core)
        away_ref[rows_at(i, TOK)] = part
        small_ref[pl.ds(8 + i, 1)] = gain
        part, gain = block(2 * i + core)
        keep_ref[rows_at(i, TOK)] = part
        small_ref[pl.ds(12 + i, 1)] = gain
        return 0

    lax.fori_loop(0, 4, step, 0)
    high, low = halves(small_ref[...])
    away_ref[4 * TOK : 4 * TOK + 16] = high
    away_ref[4 * TOK + 16 :] = low


def pair_body(at_ref, got_ref, keep_ref, small_ref, *refs):
    sends, tinies, own_ref, both_ref, gown_ref, gain_buf = (
        refs[:3], refs[3:6], refs[6], refs[7], refs[8], refs[9]
    )
    zl = places(at_ref)[0]
    got = got_ref[4 * TOK : 4 * TOK + 16].astype(F32) + got_ref[4 * TOK + 16 :].astype(F32)
    dots = small_ref[:8] + got[:8]
    both_ref[...] = dots
    high, low = halves(dots)
    gain_buf[...] = jnp.concatenate([small_ref[12:16] + got[8:12]] * 2, axis=0)

    def block(i):
        return keep_ref[rows_at(i, TOK)].astype(F32) + got_ref[rows_at(i, TOK)].astype(F32)

    def gain(i):
        return jnp.broadcast_to(gain_buf[pl.ds(i, 1)], (8, LANES))

    for d, (ref, tiny) in enumerate(zip(sends, tinies)):
        to = (zl + d + 1) % 4
        ref[:TOK] = block(to).astype(BF)
        ref[TOK : TOK + 16] = jnp.concatenate([high, low], axis=0)
        tiny[...] = jnp.concatenate(halves(gain(to)), axis=0)
    own_ref[...] = block(zl)
    gown_ref[...] = gain(zl)


def tail_of(ref, at):
    return ref[at : at + 8].astype(F32) + ref[at + 8 : at + 16].astype(F32)


def weights_body(at_ref, normed_ref, go_ref, g_ref, gown_ref, *refs):
    tinies, along_x, along_y = refs[:3], refs[3:7], refs[7:11]
    gsum_ref, wg_ref = refs[11], refs[12]
    _, _, x, _, y = places(at_ref)
    gain = gown_ref[...]
    for ref in tinies:
        gain = gain + tail_of(ref, 0)
    gsum_ref[...] = gain
    tail = jnp.concatenate(halves(gain), axis=0)

    def step(i, _):
        at = rows_at(i, 256)
        three = dot(normed_ref[:, at], g_ref[:, : 3 * LANES], 0, 0)
        last = dot(go_ref[:, at], g_ref[:, 3 * LANES :], 0, 0)
        for j in range(4):
            part = three[:, j * LANES : (j + 1) * LANES] if j < 3 else last
            wg_ref[pl.ds(8 * i, 8), rows_at(j, SIDE)] = part.astype(BF).reshape(8, SIDE, LANES)
        return 0

    lax.fori_loop(0, 4, step, 0)
    for d in range(4):
        to = (x + d) % 4
        along_x[d][: 8 * 64] = wg_ref[pl.ds(8 * to, 8), :64].reshape(8 * 64, LANES)
        if d > 0:
            along_x[d][8 * 64 :] = tail
        to = (y + d) % 4
        for i in range(8):
            along_y[d][i * 64 : (i + 1) * 64] = wg_ref[4 * i + to, 64:]


def gather_sum(refs, rows):
    acc = refs[0][:rows].astype(F32)
    for ref in refs[1:]:
        acc = acc + ref[:rows].astype(F32)
    return acc


def second_body(at_ref, gsum_ref, *refs):
    xs, ys = refs[:4], refs[4:8]
    along_y, along_x, gout_ref, one, two = refs[8:12], refs[12:16], refs[16], refs[17], refs[18]
    _, _, x, _, y = places(at_ref)
    one[...] = gather_sum(xs, 512)
    two[...] = gather_sum(ys, 512)
    gain = gsum_ref[...]
    for ref in xs[1:]:
        gain = gain + tail_of(ref, 512)
    gout_ref[...] = gain
    tail = jnp.concatenate(halves(gain), axis=0)
    for d in range(4):
        kind = along_y[d].dtype
        for zh in range(2):
            along_y[d][zh * 64 : (zh + 1) * 64] = one[
                rows_at(4 * zh + (y + d) % 4, 64)
            ].astype(kind)
        if d > 0:
            along_y[d][128:] = tail
        along_x[d][...] = two[rows_at((x + d) % 4, 128)].astype(kind)


def third_body(at_ref, gsum_ref, *refs):
    ys, xs = refs[:4], refs[4:8]
    send_ref, own_ref, gout_ref, buf = refs[8:]
    _, _, _, zh, _ = places(at_ref)
    buf[:128] = gather_sum(ys, 128)
    buf[128:] = gather_sum(xs, 128)
    gain = gsum_ref[...]
    for ref in ys[1:]:
        gain = gain + tail_of(ref, 128)
    gout_ref[...] = gain
    for half in range(2):
        at = slice(half * 64, half * 64 + 64)
        send_ref[at] = buf[rows_at(2 * half + 1 - zh, 64)].astype(BF)
        own_ref[at] = buf[rows_at(2 * half + zh, 64)]
    send_ref[128:] = jnp.concatenate(halves(gain), axis=0)


def last_body(own_ref, got_ref, gain_ref, q_ref, k_ref, v_ref, o_ref, gout_ref, *, scale):
    acc = (own_ref[...] + got_ref[:128].astype(F32)) * scale
    for j, ref in enumerate((q_ref, k_ref, v_ref)):
        ref[...] = acc[j * SIDE : (j + 1) * SIDE]
    o_ref[...] = acc[3 * SIDE :].T
    gain = (gain_ref[...] + tail_of(got_ref, 128)) * scale
    gout_ref[...] = gain[:1]


def norm_body(at_ref, x_ref, gain_ref, own_ref, r1_ref, r2_ref, r3_ref, dots_ref, inv_ref, gx_ref):
    grad = own_ref[...]
    dots = dots_ref[...]
    for ref in (r1_ref, r2_ref, r3_ref):
        grad = grad + ref[:TOK].astype(F32)
        dots = dots + tail_of(ref, TOK)
    cols = [jnp.broadcast_to(dots[i : i + 1], (LANES, LANES)).T for i in range(8)]
    row_dot = jnp.concatenate(cols, axis=0)
    x = x_ref[...].astype(F32)
    inv = inv_ref[...]
    gx = inv * gain_ref[...] * grad - x * (inv * inv) * row_dot * (1.0 / 1024)
    gx_ref[...] = gx.astype(BF)


SMEM = pl.BlockSpec(memory_space=pltpu.SMEM)
VMEM = pl.BlockSpec(memory_space=pltpu.VMEM)


def along(slab_to):
    return [(s, slab_to(s)) for s in range(SIDE)]


def to_x(d):
    return along(lambda s: (s // 8 + d) % 4 * 8 + s % 8)


def to_y(d):
    return along(lambda s: s // 4 * 4 + (s + d) % 4)


def move(a, pairs, axis="slab"):
    return lax.ppermute(a, axis, pairs)


def moved(arrays, to):
    return [move(a, to(d + 1)) for d, a in enumerate(arrays)]


def body(
    inputs, norm_gain, query_weight, key_weight, value_weight, out_weight, logit_scale, grad_output
):
    rows, width = inputs.shape
    head_dim = 64
    at = jnp.stack([lax.axis_index("head"), lax.axis_index("slab")]).astype(jnp.int32)
    factors = logit_scale / math.sqrt(head_dim)
    over_z = along(lambda s: s ^ 4)

    mine = call(
        pack_body,
        shape((SIDE, 4 * LANES), BF),
        "pack",
        in_specs=[pl.BlockSpec(memory_space=pl.ANY)] * 4,
        scratch_shapes=[
            pltpu.VMEM((LANES, SIDE), BF),
            pltpu.VMEM((3, SIDE, LANES), BF),
            pltpu.SemaphoreType.DMA((4,)),
        ],
    )(query_weight, key_weight, value_weight, out_weight)
    half = shape((2 * SIDE, 2 * LANES), BF)
    one, two = call(pair_up_body, (half, half), "pair_up", in_specs=[SMEM, VMEM, VMEM])(
        at, mine, move(mine, over_z)
    )
    got = [one] + moved([one] * 3, to_x) + [two] + moved([two] * 3, to_y)
    half = shape((8 * SIDE, 2 * LANES), BF)
    one, two = call(line_up_body, (half, half), "line_up", in_specs=[SMEM] + [VMEM] * 8)(at, *got)
    pieces = [one] + moved([one] * 3, to_y) + [two] + moved([two] * 3, to_x)

    blk = 256
    normed, inv = call(
        norm_stats_body,
        (shape((rows, width), BF), shape((rows, LANES), F32)),
        "norm_stats",
        grid=(rows // blk,),
        in_specs=[
            pl.BlockSpec((blk, width), lambda i: (i, 0)),
            pl.BlockSpec((1, width), lambda i: (0, 0)),
        ],
        out_specs=(
            pl.BlockSpec((blk, width), lambda i: (i, 0)),
            pl.BlockSpec((blk, LANES), lambda i: (i, 0)),
        ),
    )(inputs, norm_gain.reshape(1, width))
    proj, weights = call(
        project_body,
        (shape((SIDE, 4, SIDE, LANES), BF), shape((width, 4 * LANES), BF)),
        "project",
        in_specs=[SMEM] + [VMEM] * 10,
    )(at, normed, grad_output, *pieces)

    z_in = lax.all_to_all(proj, "slab", 0, 0, tiled=True)
    big = (4, SIDE, 4, 8, LANES)
    local = call(
        plane_body,
        shape(big, F32),
        "plane",
        in_specs=[VMEM, SMEM],
        scratch_shapes=[
            pltpu.VMEM(big, F32),
            pltpu.VMEM((256, 256), F32),
            pltpu.VMEM((128, 128), F32),
        ],
    )(proj, factors)
    z_terms = call(
        depth_body,
        shape((SIDE, 4, SIDE, LANES), BF),
        "depth",
        in_specs=[VMEM, SMEM],
        scratch_shapes=[
            pltpu.VMEM(big, F32),
            pltpu.VMEM(big, F32),
            pltpu.VMEM((256, 256), F32),
        ],
    )(z_in, factors)
    back = lax.all_to_all(z_terms, "slab", 0, 0, tiled=True)

    away, keep, small, grads = call(
        combine_body,
        (
            shape((4 * TOK + 32, LANES), BF),
            shape((4 * TOK, LANES), BF),
            shape((16, LANES), F32),
            shape((TOK, 4 * LANES), BF),
        ),
        "combine",
        in_specs=[SMEM] + [VMEM] * 6,
    )(at, local, back, proj, normed, norm_gain.reshape(8, LANES), weights)

    got = move(away, [(i, i ^ 1) for i in range(8)], "head")
    piece, tiny, row8 = (
        shape((TOK + 16, LANES), BF),
        shape((16, LANES), BF),
        shape((8, LANES), F32),
    )
    *sends, own, dots, gown = call(
        pair_body,
        (piece,) * 3 + (tiny,) * 3 + (shape((TOK, LANES), F32), row8, row8),
        "pair",
        in_specs=[SMEM] + [VMEM] * 3,
        scratch_shapes=[pltpu.VMEM((8, LANES), F32)],
    )(at, got, keep, small)
    to_zl = lambda d: [(i, (i + 2 * d) % 8) for i in range(8)]
    tinies = [move(s, to_zl(d + 1), "head") for d, s in enumerate(sends[3:])]
    parts = [move(s, to_zl(d + 1), "head") for d, s in enumerate(sends[:3])]

    first = shape((528, LANES), BF)
    plain = shape((512, LANES), BF)
    *sends, gsum = call(
        weights_body,
        (plain,) + (first,) * 3 + (plain,) * 4 + (row8,),
        "weight_grads",
        in_specs=[SMEM] + [VMEM] * 7,
        scratch_shapes=[pltpu.VMEM((SIDE, LANES, LANES), BF)],
    )(at, normed, grad_output, grads, gown, *tinies)
    got = [sends[0]] + moved(sends[1:4], to_x) + [sends[4]] + moved(sends[5:8], to_y)
    sq = shape((LANES, LANES), BF)
    sqf = shape((LANES, LANES), F32)
    tall = shape((LANES + 16, LANES), BF)
    *sends, gsum = call(
        second_body,
        (sqf,) + (tall,) * 3 + (sqf,) + (sq,) * 3 + (row8,),
        "slab_second",
        in_specs=[SMEM] + [VMEM] * 9,
        scratch_shapes=[pltpu.VMEM((512, LANES), F32)] * 2,
    )(at, gsum, *got)
    got = [sends[0]] + moved(sends[1:4], to_y) + [sends[4]] + moved(sends[5:8], to_x)
    send, mine, gsum = call(
        third_body,
        (tall, sqf, row8),
        "slab_third",
        in_specs=[SMEM] + [VMEM] * 9,
        scratch_shapes=[pltpu.VMEM((256, LANES), F32)],
    )(at, gsum, *got)
    part = shape((SIDE, LANES), F32)
    gqw, gkw, gvw, gow, ggain = call(
        functools.partial(last_body, scale=1.0 / math.sqrt(rows * SIDE)),
        (part, part, part, shape((LANES, SIDE), F32), shape((1, LANES), F32)),
        "slab_last",
    )(mine, move(send, over_z), gsum)

    whole = lambda dims: pl.BlockSpec(dims, lambda i, h: (0,) * len(dims))
    grad_inputs = pl.pallas_call(
        norm_body,
        out_shape=shape((rows, LANES), BF),
        name="norm_back",
        grid_spec=pltpu.PrefetchScalarGridSpec(
            num_scalar_prefetch=1,
            grid=(1,),
            in_specs=[
                pl.BlockSpec((rows, LANES), lambda i, h: (0, h[0])),
                pl.BlockSpec((1, LANES), lambda i, h: (0, h[0])),
                whole((TOK, LANES)),
                whole((TOK + 16, LANES)),
                whole((TOK + 16, LANES)),
                whole((TOK + 16, LANES)),
                whole((8, LANES)),
                whole((TOK, LANES)),
            ],
            out_specs=whole((rows, LANES)),
        ),
        compiler_params=pltpu.CompilerParams(vmem_limit_bytes=VM),
    )(at, inputs, norm_gain.reshape(1, width), own, *parts, dots, inv)
    return grad_inputs, ggain.reshape(LANES), gqw, gkw, gvw, gow


def solution(mesh):
    in_specs = (
        P("slab", None),
        P(),
        P("slab", "head"),
        P("slab", "head"),
        P("slab", "head"),
        P("head", "slab"),
        P("head"),
        P("slab", None),
    )
    out_specs = (
        P("slab", "head"),
        P("head"),
        P("slab", "head"),
        P("slab", "head"),
        P("slab", "head"),
        P("head", "slab"),
    )
    return jax.shard_map(body, mesh=mesh, in_specs=in_specs, out_specs=out_specs, check_vma=False)
```

```python
import functools
import math

import jax
import jax.numpy as jnp
from jax import lax
from jax.experimental import pallas as pl
from jax.experimental.pallas import tpu as pltpu
from jax.sharding import PartitionSpec as P


BF = jnp.bfloat16
F32 = jnp.float32
SIDE = 32
LANES = 128
TOK = SIDE * SIDE
NEG = -1e30
VM = 20 << 20


def dot(a, b, ca, cb):
    return lax.dot_general(a, b, (((ca,), (cb,)), ((), ())), preferred_element_type=F32)


def call(body, outs, **kw):
    return pl.pallas_call(
        body,
        out_shape=outs,
        compiler_params=pltpu.CompilerParams(vmem_limit_bytes=VM),
        **kw,
    )


def shape(dims, kind):
    return jax.ShapeDtypeStruct(dims, kind)


def far(dims, kind):
    return pltpu.HBM(dims, kind)


def stay(a):
    return pltpu.with_memory_space_constraint(a, pltpu.HBM)


def places(at_ref):
    head, slab = at_ref[0], at_ref[1]
    return head // 2, head % 2, slab // 8, (slab // 4) % 2, slab % 4


def rows_at(i, count):
    return pl.ds(pl.multiple_of(i * count, count), count)


def pack_body(q_ref, k_ref, v_ref, o_ref, out_ref, buf, sems):
    copies = [
        pltpu.make_async_copy(src, buf.at[j], sems.at[j])
        for j, src in enumerate((q_ref, k_ref, v_ref, o_ref))
    ]
    for c in copies:
        c.start()
    for c in copies:
        c.wait()
    for j in range(4):
        out_ref[:, j * LANES : (j + 1) * LANES] = buf[j]


def pair_up_body(at_ref, mine_ref, got_ref, out_ref):
    _, _, _, zh, _ = places(at_ref)
    for place, ref in ((zh, mine_ref), (1 - zh, got_ref)):
        out_ref[:, rows_at(place, SIDE)] = jnp.broadcast_to(ref[...][None], (16, *ref.shape))


def norm_stats_body(x_ref, gain_ref, normed_ref, inv_ref):
    x = x_ref[...].astype(F32)
    width = x.shape[1]
    inv = lax.rsqrt(jnp.sum(x * x, axis=1, keepdims=True) / width + 1e-06)
    normed_ref[...] = (x * inv * gain_ref[...]).astype(BF)
    inv_ref[...] = jnp.broadcast_to(inv, inv_ref.shape)


def project_body(normed_ref, go_ref, pieces_ref, out_ref, w_ref):
    @pl.when(pl.program_id(0) == 0)
    def _():
        for x in range(4):
            for zh in range(2):
                for y in range(4):
                    d = x * 8 + zh * 4 + y
                    w_ref[d * SIDE : (d + 1) * SIDE] = pieces_ref[
                        x * 4 + y, zh * SIDE : (zh + 1) * SIDE
                    ]

    rows = normed_ref.shape[0]
    three = dot(normed_ref[...], w_ref[:, : 3 * LANES], 1, 0)
    last = dot(go_ref[...], w_ref[:, 3 * LANES :], 1, 0)
    for j in range(4):
        part = three[:, j * LANES : (j + 1) * LANES] if j < 3 else last
        out_ref[:, j] = part.astype(BF).reshape(rows // SIDE, SIDE, LANES)


def first_head(rows):
    return lax.broadcasted_iota(jnp.int32, (rows, LANES), 1) < LANES // 2


def stacked(a):
    rows = a.shape[0]
    keep = first_head(rows)
    zero = jnp.zeros_like(a)
    return jnp.concatenate([jnp.where(keep, a, zero), jnp.where(keep, zero, a)], axis=0)


def folded(a):
    rows = a.shape[0] // 2
    return jnp.where(first_head(rows), a[:rows], a[rows:])


def attend(q, k, v, g, factors, bias):
    rows = q.shape[0]
    k2, v2 = stacked(k), stacked(v)
    s = dot(q, k2, 1, 1)
    dp = dot(g, v2, 1, 1)
    probs = []
    for h in range(2):
        sh = s[:, h * rows : (h + 1) * rows] * factors[h] + bias
        top = jnp.max(sh, axis=1, keepdims=True)
        e = jnp.exp(sh - top)
        probs.append(e / jnp.sum(e, axis=1, keepdims=True))
    pb = jnp.concatenate([p.astype(BF) for p in probs], axis=1)
    out = dot(pb, v2, 1, 0)
    go = g.astype(F32) * out
    keep = first_head(rows)
    grads = []
    for h in range(2):
        mine = jnp.where(keep, go, 0.0) if h == 0 else jnp.where(keep, 0.0, go)
        delta = jnp.sum(mine, axis=1, keepdims=True)
        dh = dp[:, h * rows : (h + 1) * rows]
        grads.append((probs[h] * (dh - delta) * factors[h]).astype(BF))
    ds = jnp.concatenate(grads, axis=1)
    gq = dot(ds, k2, 1, 0)
    gk = folded(dot(ds, q, 0, 0))
    gv = folded(dot(pb, g, 0, 0))
    return out, gq, gk, gv


def same_line(rows, line):
    a = line(lax.broadcasted_iota(jnp.int32, (rows, rows), 0))
    b = line(lax.broadcasted_iota(jnp.int32, (rows, rows), 1))
    return jnp.where(a == b, 0.0, NEG).astype(F32)


def strided_lines(in_ref, f_ref, wide_ref, bias_ref, add):
    for j in range(4):
        wide_ref[j] = in_ref[:, j].astype(F32).reshape(SIDE, 4, 8, LANES)
    rows = 8 * SIDE
    bias_ref[...] = same_line(rows, lambda i: i % 8)
    factors = (f_ref[0], f_ref[1])

    def step(b, _):
        parts = [wide_ref[j, :, b].reshape(rows, LANES).astype(BF) for j in range(4)]
        for j, r in enumerate(attend(*parts, factors, bias_ref[...])):
            add(j, b, r.reshape(SIDE, 8, LANES))
        return 0

    lax.fori_loop(0, 4, step, 0)


def plane_body(in_ref, f_ref, out_ref, wide_ref, bias_ref, bias_x_ref):
    rows = 4 * SIDE
    bias_x_ref[...] = same_line(rows, lambda i: i // SIDE)
    factors = (f_ref[0], f_ref[1])

    def step(b, _):
        parts = [in_ref[pl.ds(4 * b, 4), j].reshape(rows, LANES) for j in range(4)]
        for j, r in enumerate(attend(*parts, factors, bias_x_ref[...])):
            out_ref[j, pl.ds(4 * b, 4)] = r.reshape(4, 4, 8, LANES)
        return 0

    lax.fori_loop(0, 8, step, 0)

    def add(j, b, r):
        out_ref[j, :, b] += r

    strided_lines(in_ref, f_ref, wide_ref, bias_ref, add)


def depth_body(in_ref, f_ref, out_ref, wide_ref, res_ref, bias_ref):
    def add(j, b, r):
        res_ref[j, :, b] = r

    strided_lines(in_ref, f_ref, wide_ref, bias_ref, add)
    for j in range(4):
        out_ref[:, j] = res_ref[j].reshape(SIDE, SIDE, LANES).astype(BF)


def halves(a):
    high = a.astype(BF)
    return high, (a - high.astype(F32)).astype(BF)


def combine_body(
    at_ref, loc_ref, back_ref, proj_ref, normed_ref, gain_ref, w_ref,
    away_ref, keep_ref, small_ref, g_ref, sum_ref,
):
    core = places(at_ref)[1]
    step = pl.program_id(0)
    rows = normed_ref.shape[0]
    total = jnp.zeros((rows, LANES), F32)
    for j in range(4):
        part = loc_ref[j].reshape(rows, LANES) + back_ref[:, j].astype(F32).reshape(rows, LANES)
        part = part.astype(BF)
        at = (j - 1) % 4
        g_ref[:, at * LANES : (at + 1) * LANES] = part
        if j > 0:
            total += part.astype(F32) * proj_ref[:, j - 1].astype(F32).reshape(rows, LANES)
    for i in range(rows // LANES):
        row = jnp.sum(total[i * LANES : (i + 1) * LANES].T, axis=0, keepdims=True)
        small_ref[pl.ds(step * (rows // LANES) + i, 1)] = row

    @pl.when(step == 0)
    def _():
        sum_ref[...] = jnp.zeros_like(sum_ref)

    def block(h):
        w = w_ref[rows_at(h, LANES), : 3 * LANES]
        part = dot(g_ref[:, : 3 * LANES], w, 1, 1).astype(BF)
        n = normed_ref[:, rows_at(h, LANES)].astype(F32)
        return part, jnp.sum((part.astype(F32) * n).reshape(rows // 8, 8, LANES), axis=0)

    for i in range(4):
        away_ref[i], gain = block(2 * i + 1 - core)
        sum_ref[i] += gain
        keep_ref[i], gain = block(2 * i + core)
        sum_ref[4 + i] += gain

    @pl.when(step == pl.num_programs(0) - 1)
    def _():
        for i in range(8):
            h = 2 * (i % 4) + (1 - core if i < 4 else core)
            gain = jnp.sum(sum_ref[i], axis=0, keepdims=True) / gain_ref[pl.ds(h, 1)]
            small_ref[8 + i : 9 + i] = gain


def pair_body(at_ref, got_ref, keep_ref, small_ref, sgot_ref, *refs):
    sends, tinies, own_ref, both_ref, gown_ref, gain_buf = (
        refs[:3], refs[3:6], refs[6], refs[7], refs[8], refs[9]
    )
    zl = places(at_ref)[0]
    got = sgot_ref[...]
    dots = small_ref[:8] + got[:8]
    both_ref[...] = dots
    high, low = halves(dots)
    gain_buf[...] = jnp.concatenate([small_ref[12:16] + got[8:12]] * 2, axis=0)

    def block(i):
        return keep_ref[i].astype(F32) + got_ref[i].astype(F32)

    def gain(i):
        return jnp.broadcast_to(gain_buf[pl.ds(i, 1)], (8, LANES))

    for d, (ref, tiny) in enumerate(zip(sends, tinies)):
        to = (zl + d + 1) % 4
        ref[:TOK] = block(to).astype(BF)
        ref[TOK : TOK + 16] = jnp.concatenate([high, low], axis=0)
        tiny[...] = jnp.concatenate(halves(gain(to)), axis=0)
    own_ref[...] = block(zl)
    gown_ref[...] = gain(zl)


def tail_of(ref, at):
    return ref[at : at + 8].astype(F32) + ref[at + 8 : at + 16].astype(F32)


def weights_body(normed_ref, go_ref, g_ref, gown_ref, t1_ref, t2_ref, t3_ref, out_ref, gsum_ref):
    gain = gown_ref[...]
    for ref in (t1_ref, t2_ref, t3_ref):
        gain = gain + tail_of(ref, 0)
    gsum_ref[...] = gain
    tail = jnp.concatenate(halves(gain), axis=0)
    three = dot(normed_ref[...], g_ref[:, : 3 * LANES], 0, 0)
    last = dot(go_ref[...], g_ref[:, 3 * LANES :], 0, 0)
    for j in range(4):
        part = three[:, j * LANES : (j + 1) * LANES] if j < 3 else last
        part = part.astype(BF).reshape(2, 4, SIDE, LANES)
        for zh in range(2):
            at = zh * LANES + j * SIDE
            out_ref[:, at : at + SIDE] = part[zh]
    out_ref[:, 2 * LANES :] = jnp.broadcast_to(tail[None], (4, 16, LANES))


def plane_sum_body(at_ref, in_ref, send_ref, own_ref, gain_ref, buf):
    zh = places(at_ref)[3]
    acc = in_ref[0].astype(F32)
    for i in range(1, 16):
        acc = acc + in_ref[i].astype(F32)
    buf[...] = acc
    gain = acc[2 * LANES : 2 * LANES + 8] + acc[2 * LANES + 8 :]
    gain_ref[...] = gain
    send_ref[:LANES] = buf[rows_at(1 - zh, LANES)].astype(BF)
    send_ref[LANES:] = jnp.concatenate(halves(gain), axis=0)
    own_ref[...] = buf[rows_at(zh, LANES)]


def last_body(own_ref, got_ref, gain_ref, q_ref, k_ref, v_ref, o_ref, gout_ref, *, scale):
    acc = (own_ref[...] + got_ref[:128].astype(F32)) * scale
    for j, ref in enumerate((q_ref, k_ref, v_ref)):
        ref[...] = acc[j * SIDE : (j + 1) * SIDE]
    o_ref[...] = acc[3 * SIDE :]
    gain = (gain_ref[...] + tail_of(got_ref, 128)) * scale
    gout_ref[...] = gain[:1]


def norm_body(at_ref, x_ref, gain_ref, own_ref, r1_ref, r2_ref, r3_ref, dots_ref, inv_ref, gx_ref):
    grad = own_ref[...]
    dots = dots_ref[...]
    for ref in (r1_ref, r2_ref, r3_ref):
        grad = grad + ref[:TOK].astype(F32)
        dots = dots + tail_of(ref, TOK)
    cols = [jnp.broadcast_to(dots[i : i + 1], (LANES, LANES)).T for i in range(8)]
    row_dot = jnp.concatenate(cols, axis=0)
    x = x_ref[...].astype(F32)
    inv = inv_ref[...]
    gx = inv * gain_ref[...] * grad - x * (inv * inv) * row_dot * (1.0 / 1024)
    gx_ref[...] = gx.astype(BF)


SMEM = pl.BlockSpec(memory_space=pltpu.SMEM)
VMEM = pl.BlockSpec(memory_space=pltpu.VMEM)


PLANES = [[x * 8 + zh * 4 + y for x in range(4) for y in range(4)] for zh in range(2)]
OVER_Z = [(s, s ^ 4) for s in range(SIDE)]


def in_plane(a):
    return lax.all_to_all(a, "slab", 0, 0, tiled=True, axis_index_groups=PLANES)


def body(
    inputs, norm_gain, query_weight, key_weight, value_weight, out_weight, logit_scale, grad_output
):
    rows, width = inputs.shape
    head_dim = 64
    at = jnp.stack([lax.axis_index("head"), lax.axis_index("slab")]).astype(jnp.int32)
    factors = logit_scale / math.sqrt(head_dim)
    blk = 256
    whole = lambda dims: pl.BlockSpec(dims, lambda i: (0,) * len(dims))
    by_rows = lambda dims: pl.BlockSpec(dims, lambda i: (i,) + (0,) * (len(dims) - 1))

    mine = call(
        pack_body,
        shape((SIDE, 4 * LANES), BF),
        in_specs=[pl.BlockSpec(memory_space=pltpu.HBM)] * 4,
        scratch_shapes=[pltpu.VMEM((4, SIDE, LANES), BF), pltpu.SemaphoreType.DMA((4,))],
    )(*(stay(w) for w in (query_weight, key_weight, value_weight, out_weight.T)))
    other = lax.ppermute(mine, "slab", OVER_Z)
    spread = call(
        pair_up_body, far((16, 2 * SIDE, 4 * LANES), BF), in_specs=[SMEM, VMEM, VMEM]
    )(at, mine, other)
    normed, inv = call(
        norm_stats_body,
        (far((rows, width), BF), far((rows, LANES), F32)),
        grid=(rows // blk,),
        in_specs=[by_rows((blk, width)), whole((1, width))],
        out_specs=(by_rows((blk, width)), by_rows((blk, LANES))),
    )(inputs, norm_gain.reshape(1, width))
    pieces = in_plane(spread)

    proj, weights = call(
        project_body,
        (far((SIDE, 4, SIDE, LANES), BF), far((width, 4 * LANES), BF)),
        grid=(rows // blk,),
        in_specs=[
            by_rows((blk, width)),
            by_rows((blk, width)),
            whole((16, 2 * SIDE, 4 * LANES)),
        ],
        out_specs=(by_rows((blk // SIDE, 4, SIDE, LANES)), whole((width, 4 * LANES))),
    )(stay(normed), stay(grad_output), pieces)

    z_in = lax.all_to_all(proj, "slab", 0, 0, tiled=True)
    big = (4, SIDE, 4, 8, LANES)
    local = call(
        plane_body,
        far(big, F32),
        in_specs=[VMEM, SMEM],
        scratch_shapes=[
            pltpu.VMEM(big, F32),
            pltpu.VMEM((256, 256), F32),
            pltpu.VMEM((128, 128), F32),
        ],
    )(proj, factors)
    z_terms = call(
        depth_body,
        far((SIDE, 4, SIDE, LANES), BF),
        in_specs=[VMEM, SMEM],
        scratch_shapes=[
            pltpu.VMEM(big, F32),
            pltpu.VMEM(big, F32),
            pltpu.VMEM((256, 256), F32),
        ],
    )(z_in, factors)
    back = lax.all_to_all(z_terms, "slab", 0, 0, tiled=True)

    lines = blk // SIDE
    parts4 = pl.BlockSpec((4, blk, LANES), lambda i: (0, i, 0))
    away, keep, small, grads = call(
        combine_body,
        (
            shape((4, TOK, LANES), BF),
            shape((4, TOK, LANES), BF),
            shape((16, LANES), F32),
            shape((TOK, 4 * LANES), BF),
        ),
        grid=(rows // blk,),
        in_specs=[
            SMEM,
            pl.BlockSpec((4, lines, 4, 8, LANES), lambda i: (0, i, 0, 0, 0)),
            by_rows((lines, 4, SIDE, LANES)),
            by_rows((lines, 4, SIDE, LANES)),
            by_rows((blk, width)),
            whole((8, LANES)),
            whole((width, 4 * LANES)),
        ],
        out_specs=(parts4, parts4, whole((16, LANES)), by_rows((blk, 4 * LANES))),
        scratch_shapes=[pltpu.VMEM((8, 8, LANES), F32)],
    )(at, stay(local), back, proj, normed, norm_gain.reshape(8, LANES), stay(weights))

    swap = [(i, i ^ 1) for i in range(8)]
    got = lax.ppermute(away, "head", swap)
    got_small = lax.ppermute(small, "head", swap)
    piece, tiny, row8 = (
        shape((TOK + 16, LANES), BF),
        shape((16, LANES), BF),
        shape((8, LANES), F32),
    )
    *sends, own, dots, gown = call(
        pair_body,
        (piece,) * 3 + (tiny,) * 3 + (shape((TOK, LANES), F32), row8, row8),
        in_specs=[SMEM] + [VMEM] * 4,
        scratch_shapes=[pltpu.VMEM((8, LANES), F32)],
    )(at, got, keep, small, got_small)
    to_zl = lambda d: [(i, (i + 2 * d) % 8) for i in range(8)]
    tinies = [lax.ppermute(s, "head", to_zl(d + 1)) for d, s in enumerate(sends[3:])]
    parts = []
    for d, s in enumerate(sends[:3]):
        parts.append(lax.ppermute(s, "head", to_zl(d + 1)))

    sent, _ = call(
        weights_body,
        (shape((16, 272, LANES), BF), row8),
        grid=(4,),
        in_specs=[
            pl.BlockSpec((rows, 256), lambda i: (0, i)),
            pl.BlockSpec((rows, 256), lambda i: (0, i)),
            whole((rows, 4 * LANES)),
            whole((8, LANES)),
        ]
        + [whole((16, LANES))] * 3,
        out_specs=(by_rows((4, 272, LANES)), whole((8, LANES))),
    )(normed, grad_output, grads, gown, *tinies)
    send, mine, gain = call(
        plane_sum_body,
        (shape((LANES + 16, LANES), BF), shape((LANES, LANES), F32), row8),
        in_specs=[SMEM, VMEM],
        scratch_shapes=[pltpu.VMEM((272, LANES), F32)],
    )(at, in_plane(sent))
    part = shape((SIDE, LANES), F32)
    gqw, gkw, gvw, gow, ggain = call(
        functools.partial(last_body, scale=1.0 / math.sqrt(rows * SIDE)),
        (part, part, part, part, shape((1, LANES), F32)),
    )(mine, lax.ppermute(send, "slab", OVER_Z), gain)

    all_of = lambda dims: pl.BlockSpec(dims, lambda i, h: (0,) * len(dims))
    grad_inputs = pl.pallas_call(
        norm_body,
        out_shape=shape((rows, LANES), BF),
        name="norm_back",
        grid_spec=pltpu.PrefetchScalarGridSpec(
            num_scalar_prefetch=1,
            grid=(1,),
            in_specs=[
                pl.BlockSpec((rows, LANES), lambda i, h: (0, h[0])),
                pl.BlockSpec((1, LANES), lambda i, h: (0, h[0])),
                all_of((TOK, LANES)),
                all_of((TOK + 16, LANES)),
                all_of((TOK + 16, LANES)),
                all_of((TOK + 16, LANES)),
                all_of((8, LANES)),
                all_of((TOK, LANES)),
            ],
            out_specs=all_of((rows, LANES)),
        ),
        compiler_params=pltpu.CompilerParams(vmem_limit_bytes=VM),
    )(at, inputs, norm_gain.reshape(1, width), own, *parts, dots, inv)
    return grad_inputs, ggain.reshape(LANES), gqw, gkw, gvw, gow.T


def solution(mesh):
    in_specs = (
        P("slab", None),
        P(),
        P("slab", "head"),
        P("slab", "head"),
        P("slab", "head"),
        P("head", "slab"),
        P("head"),
        P("slab", None),
    )
    out_specs = (
        P("slab", "head"),
        P("head"),
        P("slab", "head"),
        P("slab", "head"),
        P("slab", "head"),
        P("head", "slab"),
    )

    return jax.shard_map(
        body, mesh=mesh, in_specs=in_specs, out_specs=out_specs, check_vma=False
    )
```

```python
import functools
import math

import jax
import jax.numpy as jnp
from jax import lax
from jax.experimental import pallas as pl
from jax.experimental.pallas import tpu as pltpu
from jax.sharding import PartitionSpec as P


BF = jnp.bfloat16
F32 = jnp.float32
SIDE = 32
LANES = 128
TOK = SIDE * SIDE
NEG = -1e30
VM = 20 << 20


def dot(a, b, ca, cb):
    return lax.dot_general(a, b, (((ca,), (cb,)), ((), ())), preferred_element_type=F32)


def call(body, outs, **kw):
    return pl.pallas_call(
        body,
        out_shape=outs,
        compiler_params=pltpu.CompilerParams(vmem_limit_bytes=VM),
        **kw,
    )


def shape(dims, kind):
    return jax.ShapeDtypeStruct(dims, kind)


def far(dims, kind):
    return pltpu.HBM(dims, kind)


def stay(a):
    return pltpu.with_memory_space_constraint(a, pltpu.HBM)


def places(at_ref):
    head, slab = at_ref[0], at_ref[1]
    return head // 2, head % 2, slab // 8, (slab // 4) % 2, slab % 4


def rows_at(i, count):
    return pl.ds(pl.multiple_of(i * count, count), count)


def pack_body(q_ref, k_ref, v_ref, o_ref, out_ref, buf, sems):
    copies = [
        pltpu.make_async_copy(src, buf.at[j], sems.at[j])
        for j, src in enumerate((q_ref, k_ref, v_ref, o_ref))
    ]
    for c in copies:
        c.start()
    for c in copies:
        c.wait()
    for j in range(4):
        out_ref[:, j * LANES : (j + 1) * LANES] = buf[j]


def pair_up_body(at_ref, mine_ref, got_ref, out_ref):
    _, _, _, zh, _ = places(at_ref)
    for place, ref in ((zh, mine_ref), (1 - zh, got_ref)):
        out_ref[:, rows_at(place, SIDE)] = jnp.broadcast_to(ref[...][None], (16, *ref.shape))


def norm_stats_body(x_ref, gain_ref, normed_ref, kept_ref, inv_ref):
    x = x_ref[...].astype(F32)
    width = x.shape[1]
    inv = lax.rsqrt(jnp.sum(x * x, axis=1, keepdims=True) / width + 1e-06)
    normed = (x * inv * gain_ref[...]).astype(BF)
    normed_ref[...] = normed
    kept_ref[...] = normed
    inv_ref[...] = jnp.broadcast_to(inv, inv_ref.shape)


def weights_of(pieces_ref, x):
    both = [pieces_ref[4 * x : 4 * x + 4, zh * SIDE : (zh + 1) * SIDE] for zh in range(2)]
    return jnp.concatenate([a.reshape(4 * SIDE, a.shape[-1]) for a in both], axis=0)


def project_body(normed_ref, go_ref, pieces_ref, out_ref, wout_ref, w_ref, sem):
    copy = pltpu.make_async_copy(w_ref, wout_ref, sem)

    @pl.when(pl.program_id(0) == 0)
    def _():
        for x in range(4):
            w_ref[256 * x : 256 * (x + 1)] = weights_of(pieces_ref, x)
        copy.start()

    rows = normed_ref.shape[0]
    three = dot(normed_ref[...], w_ref[:, : 3 * LANES], 1, 0)
    last = dot(go_ref[...], w_ref[:, 3 * LANES :], 1, 0)
    for j in range(4):
        part = three[:, j * LANES : (j + 1) * LANES] if j < 3 else last
        out_ref[:, j] = part.astype(BF).reshape(rows // SIDE, SIDE, LANES)

    @pl.when(pl.program_id(0) == pl.num_programs(0) - 1)
    def _():
        copy.wait()


def first_head(rows):
    return lax.broadcasted_iota(jnp.int32, (rows, LANES), 1) < LANES // 2


def stacked(a):
    rows = a.shape[0]
    keep = first_head(rows)
    zero = jnp.zeros_like(a)
    return jnp.concatenate([jnp.where(keep, a, zero), jnp.where(keep, zero, a)], axis=0)


def folded(a):
    rows = a.shape[0] // 2
    return jnp.where(first_head(rows), a[:rows], a[rows:])


def attend(q, k, v, g, factors, bias):
    rows = q.shape[0]
    k2, v2 = stacked(k), stacked(v)
    s = dot(q, k2, 1, 1)
    dp = dot(g, v2, 1, 1)
    probs = []
    for h in range(2):
        sh = s[:, h * rows : (h + 1) * rows] * factors[h] + bias
        top = jnp.max(sh, axis=1, keepdims=True)
        e = jnp.exp(sh - top)
        probs.append(e / jnp.sum(e, axis=1, keepdims=True))
    pb = jnp.concatenate([p.astype(BF) for p in probs], axis=1)
    out = dot(pb, v2, 1, 0)
    go = g.astype(F32) * out
    keep = first_head(rows)
    grads = []
    for h in range(2):
        mine = jnp.where(keep, go, 0.0) if h == 0 else jnp.where(keep, 0.0, go)
        delta = jnp.sum(mine, axis=1, keepdims=True)
        dh = dp[:, h * rows : (h + 1) * rows]
        grads.append((probs[h] * (dh - delta) * factors[h]).astype(BF))
    ds = jnp.concatenate(grads, axis=1)
    gq = dot(ds, k2, 1, 0)
    gk = folded(dot(ds, q, 0, 0))
    gv = folded(dot(pb, g, 0, 0))
    return out, gq, gk, gv


def same_line(rows, line):
    a = line(lax.broadcasted_iota(jnp.int32, (rows, rows), 0))
    b = line(lax.broadcasted_iota(jnp.int32, (rows, rows), 1))
    return jnp.where(a == b, 0.0, NEG).astype(F32)


def strided_lines(in_ref, f_ref, wide_ref, bias_ref, add):
    count = in_ref.shape[2] // 8
    for j in range(4):
        wide_ref[j] = in_ref[:, j].astype(F32).reshape(SIDE, count, 8, LANES)
    rows = 8 * SIDE
    bias_ref[...] = same_line(rows, lambda i: i % 8)
    factors = (f_ref[0], f_ref[1])

    def step(b, _):
        parts = [wide_ref[j, :, b].reshape(rows, LANES).astype(BF) for j in range(4)]
        for j, r in enumerate(attend(*parts, factors, bias_ref[...])):
            add(j, b, r.reshape(SIDE, 8, LANES))
        return 0

    lax.fori_loop(0, count, step, 0, unroll=True)


def plane_body(in_ref, f_ref, out_ref, wide_ref, bias_ref, bias_x_ref):
    rows = 4 * SIDE
    bias_x_ref[...] = same_line(rows, lambda i: i // SIDE)
    factors = (f_ref[0], f_ref[1])

    def step(b, _):
        parts = [in_ref[pl.ds(4 * b, 4), j].reshape(rows, LANES) for j in range(4)]
        for j, r in enumerate(attend(*parts, factors, bias_x_ref[...])):
            out_ref[j, pl.ds(4 * b, 4)] = r.reshape(4, 4, 8, LANES)
        return 0

    lax.fori_loop(0, 8, step, 0, unroll=4)

    def add(j, b, r):
        out_ref[j, :, b] += r

    strided_lines(in_ref, f_ref, wide_ref, bias_ref, add)


def depth_body(in_ref, f_ref, out_ref, wide_ref, res_ref, bias_ref):
    def add(j, b, r):
        res_ref[j, :, b] = r

    strided_lines(in_ref, f_ref, wide_ref, bias_ref, add)
    for j in range(4):
        out_ref[:, j] = res_ref[j].reshape(SIDE, out_ref.shape[2], LANES).astype(BF)


def halves(a):
    high = a.astype(BF)
    return high, (a - high.astype(F32)).astype(BF)


def combine_body(
    at_ref, loc_ref, back_ref, normed_ref, gain_ref, w_ref,
    away_ref, keep_ref, small_ref, g_ref, sum_ref,
):
    core = places(at_ref)[1]
    step = pl.program_id(0)
    rows = normed_ref.shape[0]
    for j in range(4):
        part = loc_ref[j].reshape(rows, LANES) + back_ref[:, j].astype(F32).reshape(rows, LANES)
        at = (j - 1) % 4
        g_ref[:, at * LANES : (at + 1) * LANES] = part.astype(BF)

    @pl.when(step == 0)
    def _():
        sum_ref[...] = jnp.zeros_like(sum_ref)

    grads = g_ref[:, : 3 * LANES]
    total = jnp.zeros((rows, LANES), F32)
    for i in range(4):
        spots = [rows_at(2 * i + core, LANES), rows_at(2 * i + 1 - core, LANES)]
        w = jnp.concatenate([w_ref[s] for s in spots], axis=0)
        part = dot(grads, w, 1, 1).astype(BF)
        keep_ref[i] = part[:, :LANES]
        away_ref[i] = part[:, LANES:]
        n = jnp.concatenate([normed_ref[:, s] for s in spots], axis=1)
        both = part.astype(F32) * n.astype(F32)
        total += both[:, :LANES] + both[:, LANES:]
        sum_ref[i] += jnp.sum(both.reshape(rows // 8, 8, 2 * LANES), axis=0)
    for i in range(rows // LANES):
        row = jnp.sum(total[i * LANES : (i + 1) * LANES].T, axis=0, keepdims=True)
        small_ref[pl.ds(step * (rows // LANES) + i, 1)] = row

    @pl.when(step == pl.num_programs(0) - 1)
    def _():
        for i in range(8):
            h = 2 * (i % 4) + (1 - core if i < 4 else core)
            both = jnp.sum(sum_ref[i % 4], axis=0, keepdims=True)
            mine = both[:, LANES:] if i < 4 else both[:, :LANES]
            small_ref[8 + i : 9 + i] = mine / gain_ref[pl.ds(h, 1)]


def pair_body(at_ref, got_ref, keep_ref, small_ref, sgot_ref, *refs):
    sends, tinies, own_ref, both_ref, gown_ref, gain_buf = (
        refs[:3], refs[3:6], refs[6], refs[7], refs[8], refs[9]
    )
    zl = places(at_ref)[0]
    got = sgot_ref[...]
    dots = small_ref[:8] + got[:8]
    both_ref[...] = dots
    high, low = halves(dots)
    gain_buf[...] = jnp.concatenate([small_ref[12:16] + got[8:12]] * 2, axis=0)

    def block(i):
        return keep_ref[i].astype(F32) + got_ref[i].astype(F32)

    def gain(i):
        return jnp.broadcast_to(gain_buf[pl.ds(i, 1)], (8, LANES))

    for d, (ref, tiny) in enumerate(zip(sends, tinies)):
        to = (zl + d + 1) % 4
        ref[:TOK] = block(to).astype(BF)
        ref[TOK : TOK + 16] = jnp.concatenate([high, low], axis=0)
        tiny[...] = jnp.concatenate(halves(gain(to)), axis=0)
    own_ref[...] = block(zl)
    gown_ref[...] = gain(zl)


def tail_of(ref, at):
    return ref[at : at + 8].astype(F32) + ref[at + 8 : at + 16].astype(F32)


def weights_body(normed_ref, go_ref, g_ref, out_ref):
    three = dot(normed_ref[...], g_ref[:, : 3 * LANES], 0, 0)
    last = dot(go_ref[...], g_ref[:, 3 * LANES :], 0, 0)
    for j in range(4):
        part = three[:, j * LANES : (j + 1) * LANES] if j < 3 else last
        part = part.astype(BF).reshape(2, 4, SIDE, LANES)
        for zh in range(2):
            at = zh * LANES + j * SIDE
            out_ref[:, at : at + SIDE] = part[zh]


def tail_body(whole_ref, gown_ref, t1_ref, t2_ref, t3_ref, out_ref, buf, sem):
    del whole_ref
    gain = gown_ref[...]
    for ref in (t1_ref, t2_ref, t3_ref):
        gain = gain + tail_of(ref, 0)
    tail = jnp.concatenate(halves(gain), axis=0)
    buf[...] = jnp.broadcast_to(tail[None], (16, 16, LANES))
    copy = pltpu.make_async_copy(buf, out_ref.at[:, 2 * LANES :], sem)
    copy.start()
    copy.wait()


def plane_sum_body(at_ref, in_ref, send_ref, own_ref, gain_ref, buf):
    zh = places(at_ref)[3]
    acc = in_ref[0].astype(F32)
    for i in range(1, 16):
        acc = acc + in_ref[i].astype(F32)
    buf[...] = acc
    gain = acc[2 * LANES : 2 * LANES + 8] + acc[2 * LANES + 8 :]
    gain_ref[...] = gain
    send_ref[:LANES] = buf[rows_at(1 - zh, LANES)].astype(BF)
    send_ref[LANES:] = jnp.concatenate(halves(gain), axis=0)
    own_ref[...] = buf[rows_at(zh, LANES)]


def last_body(own_ref, got_ref, gain_ref, q_ref, k_ref, v_ref, o_ref, gout_ref, *, scale):
    acc = (own_ref[...] + got_ref[:128].astype(F32)) * scale
    for j, ref in enumerate((q_ref, k_ref, v_ref)):
        ref[...] = acc[j * SIDE : (j + 1) * SIDE]
    o_ref[...] = acc[3 * SIDE :]
    gain = (gain_ref[...] + tail_of(got_ref, 128)) * scale
    gout_ref[...] = gain[:1]


def norm_body(at_ref, x_ref, gain_ref, own_ref, r1_ref, r2_ref, r3_ref, dots_ref, inv_ref, gx_ref):
    grad = own_ref[...]
    dots = dots_ref[...]
    for ref in (r1_ref, r2_ref, r3_ref):
        grad = grad + ref[:TOK].astype(F32)
        dots = dots + tail_of(ref, TOK)
    cols = [jnp.broadcast_to(dots[i : i + 1], (LANES, LANES)).T for i in range(8)]
    row_dot = jnp.concatenate(cols, axis=0)
    x = x_ref[...].astype(F32)
    inv = inv_ref[...]
    gx = inv * gain_ref[...] * grad - x * (inv * inv) * row_dot * (1.0 / 1024)
    gx_ref[...] = gx.astype(BF)


SMEM = pl.BlockSpec(memory_space=pltpu.SMEM)
VMEM = pl.BlockSpec(memory_space=pltpu.VMEM)


PLANES = [[x * 8 + zh * 4 + y for x in range(4) for y in range(4)] for zh in range(2)]
OVER_Z = [(s, s ^ 4) for s in range(SIDE)]


def in_plane(a):
    return lax.all_to_all(a, "slab", 0, 0, tiled=True, axis_index_groups=PLANES)


def body(
    inputs, norm_gain, query_weight, key_weight, value_weight, out_weight, logit_scale, grad_output
):
    rows, width = inputs.shape
    head_dim = 64
    at = jnp.stack([lax.axis_index("head"), lax.axis_index("slab")]).astype(jnp.int32)
    factors = logit_scale / math.sqrt(head_dim)
    blk = 256
    whole = lambda dims: pl.BlockSpec(dims, lambda i: (0,) * len(dims))
    by_rows = lambda dims: pl.BlockSpec(dims, lambda i: (i,) + (0,) * (len(dims) - 1))

    mine = call(
        pack_body,
        shape((SIDE, 4 * LANES), BF),
        in_specs=[pl.BlockSpec(memory_space=pltpu.HBM)] * 4,
        scratch_shapes=[pltpu.VMEM((4, SIDE, LANES), BF), pltpu.SemaphoreType.DMA((4,))],
    )(*(stay(w) for w in (query_weight, key_weight, value_weight, out_weight.T)))
    other = lax.ppermute(mine, "slab", OVER_Z)
    spread = call(
        pair_up_body, shape((16, 2 * SIDE, 4 * LANES), BF), in_specs=[SMEM, VMEM, VMEM]
    )(at, mine, other)
    early, normed, inv = call(
        norm_stats_body,
        (shape((rows, width), BF), far((rows, width), BF), far((rows, LANES), F32)),
        grid=(rows // blk,),
        in_specs=[by_rows((blk, width)), whole((1, width))],
        out_specs=(by_rows((blk, width)), by_rows((blk, width)), by_rows((blk, LANES))),
    )(inputs, norm_gain.reshape(1, width))
    pieces = in_plane(spread)

    proj, weights = call(
        project_body,
        (far((SIDE, 4, SIDE, LANES), BF), far((width, 4 * LANES), BF)),
        grid=(rows // blk,),
        in_specs=[
            by_rows((blk, width)),
            by_rows((blk, width)),
            whole((16, 2 * SIDE, 4 * LANES)),
        ],
        out_specs=(
            by_rows((blk // SIDE, 4, SIDE, LANES)),
            pl.BlockSpec(memory_space=pltpu.HBM),
        ),
        scratch_shapes=[pltpu.VMEM((width, 4 * LANES), BF), pltpu.SemaphoreType.DMA],
    )(early, grad_output, pieces)

    z_in = lax.all_to_all(proj, "slab", 0, 0, tiled=True)
    big = (4, SIDE, 4, 8, LANES)
    local = call(
        plane_body,
        far(big, F32),
        in_specs=[VMEM, SMEM],
        scratch_shapes=[
            pltpu.VMEM(big, F32),
            pltpu.VMEM((256, 256), F32),
            pltpu.VMEM((128, 128), F32),
        ],
    )(stay(proj), factors)
    z_terms = call(
        depth_body,
        far((SIDE, 4, SIDE, LANES), BF),
        grid=(2,),
        in_specs=[pl.BlockSpec((SIDE, 4, 16, LANES), lambda i: (0, 0, i, 0)), SMEM],
        out_specs=pl.BlockSpec((SIDE, 4, 16, LANES), lambda i: (0, 0, i, 0)),
        scratch_shapes=[
            pltpu.VMEM((4, SIDE, 2, 8, LANES), F32),
            pltpu.VMEM((4, SIDE, 2, 8, LANES), F32),
            pltpu.VMEM((256, 256), F32),
        ],
    )(z_in, factors)
    back = lax.all_to_all(z_terms, "slab", 0, 0, tiled=True)

    lines = blk // SIDE
    parts4 = pl.BlockSpec((4, blk, LANES), lambda i: (0, i, 0))
    away, keep, small, grads = call(
        combine_body,
        (
            shape((4, TOK, LANES), BF),
            shape((4, TOK, LANES), BF),
            shape((16, LANES), F32),
            shape((TOK, 4 * LANES), BF),
        ),
        grid=(rows // blk,),
        in_specs=[
            SMEM,
            pl.BlockSpec((4, lines, 4, 8, LANES), lambda i: (0, i, 0, 0, 0)),
            by_rows((lines, 4, SIDE, LANES)),
            by_rows((blk, width)),
            whole((8, LANES)),
            whole((width, 3 * LANES)),
        ],
        out_specs=(parts4, parts4, whole((16, LANES)), by_rows((blk, 4 * LANES))),
        scratch_shapes=[pltpu.VMEM((4, 8, 2 * LANES), F32)],
    )(at, stay(local), back, stay(normed), norm_gain.reshape(8, LANES), stay(weights))

    swap = [(i, i ^ 1) for i in range(8)]
    got = lax.ppermute(away, "head", swap)
    got_small = lax.ppermute(small, "head", swap)
    piece, tiny, row8 = (
        shape((TOK + 16, LANES), BF),
        shape((16, LANES), BF),
        shape((8, LANES), F32),
    )
    *sends, own, dots, gown = call(
        pair_body,
        (piece,) * 3 + (tiny,) * 3 + (shape((TOK, LANES), F32), row8, row8),
        in_specs=[SMEM] + [VMEM] * 4,
        scratch_shapes=[pltpu.VMEM((8, LANES), F32)],
    )(at, got, keep, small, got_small)
    to_zl = lambda d: [(i, (i + 2 * d) % 8) for i in range(8)]
    tinies = [lax.ppermute(s, "head", to_zl(d + 1)) for d, s in enumerate(sends[3:])]
    parts = []
    for d, s in enumerate(sends[:3]):
        parts.append(lax.ppermute(s, "head", to_zl(d + 1)))

    sent = call(
        weights_body,
        shape((16, 272, LANES), BF),
        grid=(4,),
        in_specs=[
            pl.BlockSpec((rows, 256), lambda i: (0, i)),
            pl.BlockSpec((rows, 256), lambda i: (0, i)),
            whole((rows, 4 * LANES)),
        ],
        out_specs=by_rows((4, 272, LANES)),
    )(normed, grad_output, grads)
    anywhere = pl.BlockSpec(memory_space=pl.ANY)
    sent = call(
        tail_body,
        shape((16, 272, LANES), BF),
        in_specs=[anywhere] + [VMEM] * 4,
        out_specs=anywhere,
        scratch_shapes=[pltpu.VMEM((16, 16, LANES), BF), pltpu.SemaphoreType.DMA],
        input_output_aliases={0: 0},
    )(sent, gown, *tinies)
    send, mine, gain = call(
        plane_sum_body,
        (shape((LANES + 16, LANES), BF), shape((LANES, LANES), F32), row8),
        in_specs=[SMEM, VMEM],
        scratch_shapes=[pltpu.VMEM((272, LANES), F32)],
    )(at, in_plane(sent))
    part = shape((SIDE, LANES), F32)
    gqw, gkw, gvw, gow, ggain = call(
        functools.partial(last_body, scale=1.0 / math.sqrt(rows * SIDE)),
        (part, part, part, part, shape((1, LANES), F32)),
    )(mine, lax.ppermute(send, "slab", OVER_Z), gain)

    all_of = lambda dims: pl.BlockSpec(dims, lambda i, h: (0,) * len(dims))
    grad_inputs = pl.pallas_call(
        norm_body,
        out_shape=shape((rows, LANES), BF),
        name="norm_back",
        grid_spec=pltpu.PrefetchScalarGridSpec(
            num_scalar_prefetch=1,
            grid=(1,),
            in_specs=[
                pl.BlockSpec((rows, LANES), lambda i, h: (0, h[0])),
                pl.BlockSpec((1, LANES), lambda i, h: (0, h[0])),
                all_of((TOK, LANES)),
                all_of((TOK + 16, LANES)),
                all_of((TOK + 16, LANES)),
                all_of((TOK + 16, LANES)),
                all_of((8, LANES)),
                all_of((TOK, LANES)),
            ],
            out_specs=all_of((rows, LANES)),
        ),
        compiler_params=pltpu.CompilerParams(vmem_limit_bytes=VM),
    )(at, inputs, norm_gain.reshape(1, width), own, *parts, dots, inv)
    return grad_inputs, ggain.reshape(LANES), gqw, gkw, gvw, gow.T


def solution(mesh):
    in_specs = (
        P("slab", None),
        P(),
        P("slab", "head"),
        P("slab", "head"),
        P("slab", "head"),
        P("head", "slab"),
        P("head"),
        P("slab", None),
    )
    out_specs = (
        P("slab", "head"),
        P("head"),
        P("slab", "head"),
        P("slab", "head"),
        P("slab", "head"),
        P("head", "slab"),
    )

    return jax.shard_map(
        body, mesh=mesh, in_specs=in_specs, out_specs=out_specs, check_vma=False
    )
```

```python
import functools
import math

import jax
import jax.numpy as jnp
from jax import lax
from jax.experimental import pallas as pl
from jax.experimental.pallas import tpu as pltpu
from jax.sharding import PartitionSpec as P


BF = jnp.bfloat16
F32 = jnp.float32
SIDE = 32
LANES = 128
TOK = SIDE * SIDE
NEG = -1e30
VM = 20 << 20


def dot(a, b, ca, cb):
    return lax.dot_general(a, b, (((ca,), (cb,)), ((), ())), preferred_element_type=F32)


def call(body, outs, **kw):
    return pl.pallas_call(
        body,
        out_shape=outs,
        compiler_params=pltpu.CompilerParams(vmem_limit_bytes=VM),
        **kw,
    )


def shape(dims, kind):
    return jax.ShapeDtypeStruct(dims, kind)


def far(dims, kind):
    return pltpu.HBM(dims, kind)


def stay(a):
    return pltpu.with_memory_space_constraint(a, pltpu.HBM)


def places(at_ref):
    head, slab = at_ref[0], at_ref[1]
    return head // 2, head % 2, slab // 8, (slab // 4) % 2, slab % 4


def rows_at(i, count):
    return pl.ds(pl.multiple_of(i * count, count), count)


def pack_body(q_ref, k_ref, v_ref, o_ref, out_ref, buf, sems):
    copies = [
        pltpu.make_async_copy(src, buf.at[j], sems.at[j])
        for j, src in enumerate((q_ref, k_ref, v_ref, o_ref))
    ]
    for c in copies:
        c.start()
    for c in copies:
        c.wait()
    for j in range(4):
        out_ref[:, j * LANES : (j + 1) * LANES] = buf[j]


def pair_up_body(at_ref, mine_ref, got_ref, out_ref):
    _, _, _, zh, _ = places(at_ref)
    for place, ref in ((zh, mine_ref), (1 - zh, got_ref)):
        out_ref[:, rows_at(place, SIDE)] = jnp.broadcast_to(ref[...][None], (16, *ref.shape))


def norm_stats_body(x_ref, gain_ref, normed_ref, kept_ref, inv_ref):
    x = x_ref[...].astype(F32)
    width = x.shape[1]
    inv = lax.rsqrt(jnp.sum(x * x, axis=1, keepdims=True) / width + 1e-06)
    normed = (x * inv * gain_ref[...]).astype(BF)
    normed_ref[...] = normed
    kept_ref[...] = normed
    inv_ref[...] = jnp.broadcast_to(inv, inv_ref.shape)


def weights_of(pieces_ref, x):
    both = [pieces_ref[4 * x : 4 * x + 4, zh * SIDE : (zh + 1) * SIDE] for zh in range(2)]
    return jnp.concatenate([a.reshape(4 * SIDE, a.shape[-1]) for a in both], axis=0)


def project_body(normed_ref, go_ref, pieces_ref, out_ref, wout_ref, w_ref, sem):
    copy = pltpu.make_async_copy(w_ref, wout_ref, sem)

    @pl.when(pl.program_id(0) == 0)
    def _():
        for x in range(4):
            w_ref[256 * x : 256 * (x + 1)] = weights_of(pieces_ref, x)
        copy.start()

    rows = normed_ref.shape[0]
    three = dot(normed_ref[...], w_ref[:, : 3 * LANES], 1, 0)
    last = dot(go_ref[...], w_ref[:, 3 * LANES :], 1, 0)
    for j in range(4):
        part = three[:, j * LANES : (j + 1) * LANES] if j < 3 else last
        out_ref[:, j] = part.astype(BF).reshape(rows // SIDE, SIDE, LANES)

    @pl.when(pl.program_id(0) == pl.num_programs(0) - 1)
    def _():
        copy.wait()


def first_head(rows):
    return lax.broadcasted_iota(jnp.int32, (rows, LANES), 1) < LANES // 2


def stacked(a):
    rows = a.shape[0]
    keep = first_head(rows)
    zero = jnp.zeros_like(a)
    return jnp.concatenate([jnp.where(keep, a, zero), jnp.where(keep, zero, a)], axis=0)


def folded(a):
    rows = a.shape[0] // 2
    return jnp.where(first_head(rows), a[:rows], a[rows:])


def attend(blocks, factors, bias):
    rows = bias.shape[0]
    keep = first_head(rows)
    cut = [slice(0, rows), slice(rows, 2 * rows)]
    k2 = [stacked(k) for _, k, _, _ in blocks]
    v2 = [stacked(v) for _, _, v, _ in blocks]
    s = [dot(blk[0], k, 1, 1) for blk, k in zip(blocks, k2)]
    dp = [dot(blk[3], v, 1, 1) for blk, v in zip(blocks, v2)]
    s = [[m[:, c] * f + bias for c, f in zip(cut, factors)] for m in s]
    top = [[jnp.max(m, axis=1, keepdims=True) for m in pair] for pair in s]
    e = [[jnp.exp(m - t) for m, t in zip(*both)] for both in zip(s, top)]
    total = [[1.0 / jnp.sum(m, axis=1, keepdims=True) for m in pair] for pair in e]
    p = [[m * t for m, t in zip(*both)] for both in zip(e, total)]
    pb = [jnp.concatenate([m.astype(BF) for m in pair], axis=1) for pair in p]
    out = [dot(m, v, 1, 0) for m, v in zip(pb, v2)]
    go = [blk[3].astype(F32) * o for blk, o in zip(blocks, out)]
    delta = [
        [
            jnp.sum(jnp.where(keep, m, 0.0), axis=1, keepdims=True),
            jnp.sum(jnp.where(keep, 0.0, m), axis=1, keepdims=True),
        ]
        for m in go
    ]
    ds = [
        jnp.concatenate(
            [
                (ph * (d[:, c] - t) * f).astype(BF)
                for ph, t, c, f in zip(pair, deltas, cut, factors)
            ],
            axis=1,
        )
        for pair, d, deltas in zip(p, dp, delta)
    ]
    gv = [folded(dot(m, blk[3], 0, 0)) for m, blk in zip(pb, blocks)]
    gq = [dot(m, k, 1, 0) for m, k in zip(ds, k2)]
    gk = [folded(dot(m, blk[0], 0, 0)) for m, blk in zip(ds, blocks)]
    return list(zip(out, gq, gk, gv))


def same_line(rows, line):
    a = line(lax.broadcasted_iota(jnp.int32, (rows, rows), 0))
    b = line(lax.broadcasted_iota(jnp.int32, (rows, rows), 1))
    return jnp.where(a == b, 0.0, NEG).astype(F32)


def strided_lines(in_ref, f_ref, wide_ref, bias_ref, add):
    count = in_ref.shape[2] // 8
    for j in range(4):
        wide_ref[j] = in_ref[:, j].astype(F32).reshape(SIDE, count, 8, LANES)
    rows = 8 * SIDE
    bias_ref[...] = same_line(rows, lambda i: i % 8)
    factors = (f_ref[0], f_ref[1])

    def step(b, _):
        parts = [wide_ref[j, :, b].reshape(rows, LANES).astype(BF) for j in range(4)]
        for j, r in enumerate(attend([parts], factors, bias_ref[...])[0]):
            add(j, b, r.reshape(SIDE, 8, LANES))
        return 0

    lax.fori_loop(0, count, step, 0, unroll=True)


def plane_body(in_ref, f_ref, out_ref, wide_ref, bias_ref, bias_x_ref):
    rows = 4 * SIDE
    bias_x_ref[...] = same_line(rows, lambda i: i // SIDE)
    factors = (f_ref[0], f_ref[1])

    def step(b, _):
        parts = [in_ref[pl.ds(4 * b, 4), j].reshape(rows, LANES) for j in range(4)]
        for j, r in enumerate(attend([parts], factors, bias_x_ref[...])[0]):
            out_ref[j, pl.ds(4 * b, 4)] = r.reshape(4, 4, 8, LANES)
        return 0

    lax.fori_loop(0, 8, step, 0, unroll=4)

    def add(j, b, r):
        out_ref[j, :, b] += r

    strided_lines(in_ref, f_ref, wide_ref, bias_ref, add)


def depth_body(in_ref, f_ref, out_ref, flat_ref, res_ref, bias_ref):
    across = in_ref.shape[2]
    for j in range(4):
        flat_ref[j] = in_ref[:, j].astype(F32).reshape(SIDE * across, LANES)
    bias_ref[...] = same_line(4 * SIDE, lambda i: i // SIDE)
    factors = (f_ref[0], f_ref[1])
    spots = [[pl.ds(4 * b + i, SIDE, across) for i in range(4)] for b in range(across // 4)]
    blocks = [
        [jnp.concatenate([flat_ref[j, s] for s in four], axis=0).astype(BF) for j in range(4)]
        for four in spots
    ]
    for four, results in zip(spots, attend(blocks, factors, bias_ref[...])):
        for j, r in enumerate(results):
            for i, s in enumerate(four):
                res_ref[j, s] = r[i * SIDE : (i + 1) * SIDE]
    for j in range(4):
        out_ref[:, j] = res_ref[j].reshape(SIDE, across, LANES).astype(BF)


def halves(a):
    high = a.astype(BF)
    return high, (a - high.astype(F32)).astype(BF)


def combine_body(
    at_ref, loc_ref, back_ref, normed_ref, gain_ref, w_ref,
    away_ref, keep_ref, small_ref, g_ref, kept_ref, sum_ref,
):
    core = places(at_ref)[1]
    step = pl.program_id(0)
    rows = normed_ref.shape[0]
    kept_ref[...] = normed_ref[...]
    for j in range(4):
        part = loc_ref[j].reshape(rows, LANES) + back_ref[:, j].astype(F32).reshape(rows, LANES)
        at = (j - 1) % 4
        g_ref[:, at * LANES : (at + 1) * LANES] = part.astype(BF)

    @pl.when(step == 0)
    def _():
        sum_ref[...] = jnp.zeros_like(sum_ref)

    grads = g_ref[:, : 3 * LANES]
    total = jnp.zeros((rows, LANES), F32)
    for i in range(4):
        spots = [rows_at(2 * i + core, LANES), rows_at(2 * i + 1 - core, LANES)]
        w = jnp.concatenate([w_ref[s] for s in spots], axis=0)
        part = dot(grads, w, 1, 1).astype(BF)
        keep_ref[i] = part[:, :LANES]
        away_ref[i] = part[:, LANES:]
        n = jnp.concatenate([normed_ref[:, s] for s in spots], axis=1)
        both = part.astype(F32) * n.astype(F32)
        total += both[:, :LANES] + both[:, LANES:]
        sum_ref[i] += jnp.sum(both.reshape(rows // 8, 8, 2 * LANES), axis=0)
    for i in range(rows // LANES):
        row = jnp.sum(total[i * LANES : (i + 1) * LANES].T, axis=0, keepdims=True)
        small_ref[pl.ds(step * (rows // LANES) + i, 1)] = row

    @pl.when(step == pl.num_programs(0) - 1)
    def _():
        for i in range(8):
            h = 2 * (i % 4) + (1 - core if i < 4 else core)
            both = jnp.sum(sum_ref[i % 4], axis=0, keepdims=True)
            mine = both[:, LANES:] if i < 4 else both[:, :LANES]
            small_ref[8 + i : 9 + i] = mine / gain_ref[pl.ds(h, 1)]


def pair_body(at_ref, got_ref, keep_ref, small_ref, sgot_ref, *refs):
    sends, tinies, own_ref, both_ref, gown_ref, gain_buf = (
        refs[:3], refs[3:6], refs[6], refs[7], refs[8], refs[9]
    )
    zl = places(at_ref)[0]
    got = sgot_ref[...]
    dots = small_ref[:8] + got[:8]
    both_ref[...] = dots
    high, low = halves(dots)
    gain_buf[...] = jnp.concatenate([small_ref[12:16] + got[8:12]] * 2, axis=0)

    def block(i):
        return keep_ref[i].astype(F32) + got_ref[i].astype(F32)

    def gain(i):
        return jnp.broadcast_to(gain_buf[pl.ds(i, 1)], (8, LANES))

    for d, (ref, tiny) in enumerate(zip(sends, tinies)):
        to = (zl + d + 1) % 4
        ref[:TOK] = block(to).astype(BF)
        ref[TOK : TOK + 16] = jnp.concatenate([high, low], axis=0)
        tiny[...] = jnp.concatenate(halves(gain(to)), axis=0)
    own_ref[...] = block(zl)
    gown_ref[...] = gain(zl)


def tail_of(ref, at):
    return ref[at : at + 8].astype(F32) + ref[at + 8 : at + 16].astype(F32)


def weights_body(normed_ref, go_ref, g_ref, out_ref):
    three = dot(normed_ref[...], g_ref[:, : 3 * LANES], 0, 0)
    last = dot(go_ref[...], g_ref[:, 3 * LANES :], 0, 0)
    for j in range(4):
        part = three[:, j * LANES : (j + 1) * LANES] if j < 3 else last
        part = part.astype(BF).reshape(2, 2, 4, SIDE, LANES)
        for x in range(2):
            for zh in range(2):
                at = zh * LANES + j * SIDE
                out_ref[4 * x : 4 * x + 4, at : at + SIDE] = part[x, zh]


def tail_body(whole_ref, gown_ref, t1_ref, t2_ref, t3_ref, out_ref, buf, sem):
    del whole_ref
    gain = gown_ref[...]
    for ref in (t1_ref, t2_ref, t3_ref):
        gain = gain + tail_of(ref, 0)
    tail = jnp.concatenate(halves(gain), axis=0)
    buf[...] = jnp.broadcast_to(tail[None], (16, 16, LANES))
    copy = pltpu.make_async_copy(buf, out_ref.at[:, 2 * LANES :], sem)
    copy.start()
    copy.wait()


def sum_over(in_ref, at):
    acc = in_ref[0, at].astype(F32)
    for i in range(1, 16):
        acc = acc + in_ref[i, at].astype(F32)
    return acc


def plane_sum_body(at_ref, in_ref, send_ref, gain_ref):
    zh = places(at_ref)[3]
    gain = sum_over(in_ref, slice(2 * LANES, 2 * LANES + 16))
    gain = gain[:8] + gain[8:]
    gain_ref[...] = gain
    send_ref[:LANES] = sum_over(in_ref, rows_at(1 - zh, LANES)).astype(BF)
    send_ref[LANES:] = jnp.concatenate(halves(gain), axis=0)


def own_sum_body(at_ref, in_ref, own_ref):
    own_ref[...] = sum_over(in_ref, rows_at(places(at_ref)[3], LANES))


def last_body(own_ref, got_ref, gain_ref, q_ref, k_ref, v_ref, o_ref, gout_ref, *, scale):
    acc = (own_ref[...] + got_ref[:128].astype(F32)) * scale
    for j, ref in enumerate((q_ref, k_ref, v_ref)):
        ref[...] = acc[j * SIDE : (j + 1) * SIDE]
    o_ref[...] = acc[3 * SIDE :]
    gain = (gain_ref[...] + tail_of(got_ref, 128)) * scale
    gout_ref[...] = gain[:1]


def norm_body(at_ref, x_ref, gain_ref, own_ref, r1_ref, r2_ref, r3_ref, dots_ref, inv_ref, gx_ref):
    grad = own_ref[...]
    dots = dots_ref[...]
    for ref in (r1_ref, r2_ref, r3_ref):
        grad = grad + ref[:TOK].astype(F32)
        dots = dots + tail_of(ref, TOK)
    cols = [jnp.broadcast_to(dots[i : i + 1], (LANES, LANES)).T for i in range(8)]
    row_dot = jnp.concatenate(cols, axis=0)
    x = x_ref[...].astype(F32)
    inv = inv_ref[...]
    gx = inv * gain_ref[...] * grad - x * (inv * inv) * row_dot * (1.0 / 1024)
    gx_ref[...] = gx.astype(BF)


SMEM = pl.BlockSpec(memory_space=pltpu.SMEM)
VMEM = pl.BlockSpec(memory_space=pltpu.VMEM)


PLANES = [[x * 8 + zh * 4 + y for x in range(4) for y in range(4)] for zh in range(2)]
OVER_Z = [(s, s ^ 4) for s in range(SIDE)]


def in_plane(a):
    return lax.all_to_all(a, "slab", 0, 0, tiled=True, axis_index_groups=PLANES)


def body(
    inputs, norm_gain, query_weight, key_weight, value_weight, out_weight, logit_scale, grad_output
):
    rows, width = inputs.shape
    head_dim = 64
    at = jnp.stack([lax.axis_index("head"), lax.axis_index("slab")]).astype(jnp.int32)
    factors = logit_scale / math.sqrt(head_dim)
    blk = 256
    whole = lambda dims: pl.BlockSpec(dims, lambda i: (0,) * len(dims))
    by_rows = lambda dims: pl.BlockSpec(dims, lambda i: (i,) + (0,) * (len(dims) - 1))

    mine = call(
        pack_body,
        shape((SIDE, 4 * LANES), BF),
        in_specs=[pl.BlockSpec(memory_space=pltpu.HBM)] * 4,
        scratch_shapes=[pltpu.VMEM((4, SIDE, LANES), BF), pltpu.SemaphoreType.DMA((4,))],
    )(*(stay(w) for w in (query_weight, key_weight, value_weight, out_weight.T)))
    other = lax.ppermute(mine, "slab", OVER_Z)
    spread = call(
        pair_up_body, shape((16, 2 * SIDE, 4 * LANES), BF), in_specs=[SMEM, VMEM, VMEM]
    )(at, mine, other)
    early, normed, inv = call(
        norm_stats_body,
        (shape((rows, width), BF), far((rows, width), BF), far((rows, LANES), F32)),
        grid=(rows // blk,),
        in_specs=[by_rows((blk, width)), whole((1, width))],
        out_specs=(by_rows((blk, width)), by_rows((blk, width)), by_rows((blk, LANES))),
    )(inputs, norm_gain.reshape(1, width))
    pieces = in_plane(spread)

    wide = 2 * blk
    proj, weights = call(
        project_body,
        (far((SIDE, 4, SIDE, LANES), BF), far((width, 4 * LANES), BF)),
        grid=(rows // wide,),
        in_specs=[
            by_rows((wide, width)),
            by_rows((wide, width)),
            whole((16, 2 * SIDE, 4 * LANES)),
        ],
        out_specs=(
            by_rows((wide // SIDE, 4, SIDE, LANES)),
            pl.BlockSpec(memory_space=pltpu.HBM),
        ),
        scratch_shapes=[pltpu.VMEM((width, 4 * LANES), BF), pltpu.SemaphoreType.DMA],
    )(early, grad_output, pieces)

    z_in = lax.all_to_all(proj, "slab", 0, 0, tiled=True)
    big = (4, SIDE, 4, 8, LANES)
    local = call(
        plane_body,
        far(big, F32),
        in_specs=[VMEM, SMEM],
        scratch_shapes=[
            pltpu.VMEM(big, F32),
            pltpu.VMEM((256, 256), F32),
            pltpu.VMEM((128, 128), F32),
        ],
    )(stay(proj), factors)
    z_terms = call(
        depth_body,
        far((SIDE, 4, SIDE, LANES), BF),
        grid=(2,),
        in_specs=[pl.BlockSpec((SIDE, 4, 16, LANES), lambda i: (0, 0, i, 0)), SMEM],
        out_specs=pl.BlockSpec((SIDE, 4, 16, LANES), lambda i: (0, 0, i, 0)),
        scratch_shapes=[
            pltpu.VMEM((4, SIDE * 16, LANES), F32),
            pltpu.VMEM((4, SIDE * 16, LANES), F32),
            pltpu.VMEM((128, 128), F32),
        ],
    )(z_in, factors)
    back = lax.all_to_all(z_terms, "slab", 0, 0, tiled=True)

    lines = blk // SIDE
    parts4 = pl.BlockSpec((4, blk, LANES), lambda i: (0, i, 0))
    away, keep, small, grads, early = call(
        combine_body,
        (
            shape((4, TOK, LANES), BF),
            shape((4, TOK, LANES), BF),
            shape((16, LANES), F32),
            shape((TOK, 4 * LANES), BF),
            shape((rows, width), BF),
        ),
        grid=(rows // blk,),
        in_specs=[
            SMEM,
            pl.BlockSpec((4, lines, 4, 8, LANES), lambda i: (0, i, 0, 0, 0)),
            by_rows((lines, 4, SIDE, LANES)),
            by_rows((blk, width)),
            whole((8, LANES)),
            whole((width, 3 * LANES)),
        ],
        out_specs=(
            parts4,
            parts4,
            whole((16, LANES)),
            by_rows((blk, 4 * LANES)),
            by_rows((blk, width)),
        ),
        scratch_shapes=[pltpu.VMEM((4, 8, 2 * LANES), F32)],
    )(at, stay(local), back, stay(normed), norm_gain.reshape(8, LANES), stay(weights))

    swap = [(i, i ^ 1) for i in range(8)]
    got = lax.ppermute(away, "head", swap)
    got_small = lax.ppermute(small, "head", swap)
    piece, tiny, row8 = (
        shape((TOK + 16, LANES), BF),
        shape((16, LANES), BF),
        shape((8, LANES), F32),
    )
    *sends, own, dots, gown = call(
        pair_body,
        (piece,) * 3 + (tiny,) * 3 + (shape((TOK, LANES), F32), row8, row8),
        in_specs=[SMEM] + [VMEM] * 4,
        scratch_shapes=[pltpu.VMEM((8, LANES), F32)],
    )(at, got, keep, small, got_small)
    to_zl = lambda d: [(i, (i + 2 * d) % 8) for i in range(8)]
    tinies = [lax.ppermute(s, "head", to_zl(d + 1)) for d, s in enumerate(sends[3:])]
    parts = []
    for d, s in enumerate(sends[:3]):
        parts.append(lax.ppermute(s, "head", to_zl(d + 1)))

    sent = call(
        weights_body,
        shape((16, 272, LANES), BF),
        grid=(2,),
        in_specs=[
            pl.BlockSpec((rows, 512), lambda i: (0, i)),
            pl.BlockSpec((rows, 512), lambda i: (0, i)),
            whole((rows, 4 * LANES)),
        ],
        out_specs=by_rows((8, 272, LANES)),
    )(early, grad_output, grads)
    anywhere = pl.BlockSpec(memory_space=pl.ANY)
    sent = call(
        tail_body,
        shape((16, 272, LANES), BF),
        in_specs=[anywhere] + [VMEM] * 4,
        out_specs=anywhere,
        scratch_shapes=[pltpu.VMEM((16, 16, LANES), BF), pltpu.SemaphoreType.DMA],
        input_output_aliases={0: 0},
    )(sent, gown, *tinies)
    pieces = in_plane(sent)
    send, gain = call(
        plane_sum_body, (shape((LANES + 16, LANES), BF), row8), in_specs=[SMEM, VMEM]
    )(at, pieces)
    other = lax.ppermute(send, "slab", OVER_Z)
    mine = call(
        own_sum_body, shape((LANES, LANES), F32), in_specs=[SMEM, VMEM]
    )(at, pieces)
    part = shape((SIDE, LANES), F32)
    gqw, gkw, gvw, gow, ggain = call(
        functools.partial(last_body, scale=1.0 / math.sqrt(rows * SIDE)),
        (part, part, part, part, shape((1, LANES), F32)),
    )(mine, other, gain)

    all_of = lambda dims: pl.BlockSpec(dims, lambda i, h: (0,) * len(dims))
    grad_inputs = pl.pallas_call(
        norm_body,
        out_shape=shape((rows, LANES), BF),
        name="norm_back",
        grid_spec=pltpu.PrefetchScalarGridSpec(
            num_scalar_prefetch=1,
            grid=(1,),
            in_specs=[
                pl.BlockSpec((rows, LANES), lambda i, h: (0, h[0])),
                pl.BlockSpec((1, LANES), lambda i, h: (0, h[0])),
                all_of((TOK, LANES)),
                all_of((TOK + 16, LANES)),
                all_of((TOK + 16, LANES)),
                all_of((TOK + 16, LANES)),
                all_of((8, LANES)),
                all_of((TOK, LANES)),
            ],
            out_specs=all_of((rows, LANES)),
        ),
        compiler_params=pltpu.CompilerParams(vmem_limit_bytes=VM),
    )(at, inputs, norm_gain.reshape(1, width), own, *parts, dots, inv)
    return grad_inputs, ggain.reshape(LANES), gqw, gkw, gvw, gow.T


def solution(mesh):
    in_specs = (
        P("slab", None),
        P(),
        P("slab", "head"),
        P("slab", "head"),
        P("slab", "head"),
        P("head", "slab"),
        P("head"),
        P("slab", None),
    )
    out_specs = (
        P("slab", "head"),
        P("head"),
        P("slab", "head"),
        P("slab", "head"),
        P("slab", "head"),
        P("head", "slab"),
    )

    return jax.shard_map(
        body, mesh=mesh, in_specs=in_specs, out_specs=out_specs, check_vma=False
    )
```

```python
import functools
import math

import jax
import jax.numpy as jnp
from jax import lax
from jax.experimental import pallas as pl
from jax.experimental.pallas import tpu as pltpu
from jax.sharding import PartitionSpec as P


BF = jnp.bfloat16
F32 = jnp.float32
SIDE = 32
LANES = 128
TOK = SIDE * SIDE
NEG = -1e30
VM = 20 << 20


def dot(a, b, ca, cb):
    return lax.dot_general(a, b, (((ca,), (cb,)), ((), ())), preferred_element_type=F32)


def call(body, outs, **kw):
    return pl.pallas_call(
        body,
        out_shape=outs,
        compiler_params=pltpu.CompilerParams(vmem_limit_bytes=VM),
        **kw,
    )


def shape(dims, kind):
    return jax.ShapeDtypeStruct(dims, kind)


def far(dims, kind):
    return pltpu.HBM(dims, kind)


def stay(a):
    return pltpu.with_memory_space_constraint(a, pltpu.HBM)


def places(at_ref):
    head, slab = at_ref[0], at_ref[1]
    return head // 2, head % 2, slab // 8, (slab // 4) % 2, slab % 4


def rows_at(i, count):
    return pl.ds(pl.multiple_of(i * count, count), count)


def pack_body(q_ref, k_ref, v_ref, o_ref, out_ref, buf, sems):
    copies = [
        pltpu.make_async_copy(src, buf.at[j], sems.at[j])
        for j, src in enumerate((q_ref, k_ref, v_ref, o_ref))
    ]
    for c in copies:
        c.start()
    for c in copies:
        c.wait()
    for j in range(4):
        out_ref[:, j * LANES : (j + 1) * LANES] = buf[j]


def pair_up_body(at_ref, mine_ref, got_ref, out_ref):
    _, _, _, zh, _ = places(at_ref)
    for place, ref in ((zh, mine_ref), (1 - zh, got_ref)):
        out_ref[:, rows_at(place, SIDE)] = jnp.broadcast_to(ref[...][None], (16, *ref.shape))


def norm_stats_body(x_ref, gain_ref, normed_ref, kept_ref, inv_ref):
    x = x_ref[...].astype(F32)
    width = x.shape[1]
    inv = lax.rsqrt(jnp.sum(x * x, axis=1, keepdims=True) / width + 1e-06)
    normed = (x * inv * gain_ref[...]).astype(BF)
    normed_ref[...] = normed
    kept_ref[...] = normed
    inv_ref[...] = jnp.broadcast_to(inv, inv_ref.shape)


def weights_of(pieces_ref, x):
    both = [pieces_ref[4 * x : 4 * x + 4, zh * SIDE : (zh + 1) * SIDE] for zh in range(2)]
    return jnp.concatenate([a.reshape(4 * SIDE, a.shape[-1]) for a in both], axis=0)


def project_body(normed_ref, go_ref, pieces_ref, out_ref, wout_ref, w_ref, sem):
    copy = pltpu.make_async_copy(w_ref, wout_ref, sem)

    @pl.when(pl.program_id(0) == 0)
    def _():
        for x in range(4):
            w_ref[256 * x : 256 * (x + 1)] = weights_of(pieces_ref, x)
        copy.start()

    rows = normed_ref.shape[0]
    three = dot(normed_ref[...], w_ref[:, : 3 * LANES], 1, 0)
    last = dot(go_ref[...], w_ref[:, 3 * LANES :], 1, 0)
    for j in range(4):
        part = three[:, j * LANES : (j + 1) * LANES] if j < 3 else last
        part = part.astype(BF).reshape(rows // 256, 2, 4, SIDE, LANES)
        for zh in range(2):
            out_ref[zh, :, :, j] = part[:, zh]

    @pl.when(pl.program_id(0) == pl.num_programs(0) - 1)
    def _():
        copy.wait()


def first_head(rows):
    return lax.broadcasted_iota(jnp.int32, (rows, LANES), 1) < LANES // 2


def stacked(a):
    rows = a.shape[0]
    keep = first_head(rows)
    zero = jnp.zeros_like(a)
    return jnp.concatenate([jnp.where(keep, a, zero), jnp.where(keep, zero, a)], axis=0)


def folded(a):
    rows = a.shape[0] // 2
    return jnp.where(first_head(rows), a[:rows], a[rows:])


def attend(blocks, factors, bias):
    rows = bias.shape[0]
    keep = first_head(rows)
    cut = [slice(0, rows), slice(rows, 2 * rows)]
    k2 = [stacked(k) for _, k, _, _ in blocks]
    v2 = [stacked(v) for _, _, v, _ in blocks]
    s = [dot(blk[0], k, 1, 1) for blk, k in zip(blocks, k2)]
    dp = [dot(blk[3], v, 1, 1) for blk, v in zip(blocks, v2)]
    s = [[m[:, c] * f + bias for c, f in zip(cut, factors)] for m in s]
    top = [[jnp.max(m, axis=1, keepdims=True) for m in pair] for pair in s]
    e = [[jnp.exp(m - t) for m, t in zip(*both)] for both in zip(s, top)]
    total = [[1.0 / jnp.sum(m, axis=1, keepdims=True) for m in pair] for pair in e]
    p = [[m * t for m, t in zip(*both)] for both in zip(e, total)]
    pb = [jnp.concatenate([m.astype(BF) for m in pair], axis=1) for pair in p]
    out = [dot(m, v, 1, 0) for m, v in zip(pb, v2)]
    go = [blk[3].astype(F32) * o for blk, o in zip(blocks, out)]
    delta = [
        [
            jnp.sum(jnp.where(keep, m, 0.0), axis=1, keepdims=True),
            jnp.sum(jnp.where(keep, 0.0, m), axis=1, keepdims=True),
        ]
        for m in go
    ]
    ds = [
        jnp.concatenate(
            [
                (ph * (d[:, c] - t) * f).astype(BF)
                for ph, t, c, f in zip(pair, deltas, cut, factors)
            ],
            axis=1,
        )
        for pair, d, deltas in zip(p, dp, delta)
    ]
    gv = [folded(dot(m, blk[3], 0, 0)) for m, blk in zip(pb, blocks)]
    gq = [dot(m, k, 1, 0) for m, k in zip(ds, k2)]
    gk = [folded(dot(m, blk[0], 0, 0)) for m, blk in zip(ds, blocks)]
    return list(zip(out, gq, gk, gv))


def same_line(rows, line):
    a = line(lax.broadcasted_iota(jnp.int32, (rows, rows), 0))
    b = line(lax.broadcasted_iota(jnp.int32, (rows, rows), 1))
    return jnp.where(a == b, 0.0, NEG).astype(F32)


def strided_lines(in_ref, f_ref, wide_ref, bias_ref, add):
    count = in_ref.shape[2] // 8
    for j in range(4):
        wide_ref[j] = in_ref[:, j].astype(F32).reshape(SIDE, count, 8, LANES)
    rows = 8 * SIDE
    bias_ref[...] = same_line(rows, lambda i: i % 8)
    factors = (f_ref[0], f_ref[1])

    def step(b, _):
        parts = [wide_ref[j, :, b].reshape(rows, LANES).astype(BF) for j in range(4)]
        for j, r in enumerate(attend([parts], factors, bias_ref[...])[0]):
            add(j, b, r.reshape(SIDE, 8, LANES))
        return 0

    lax.fori_loop(0, count, step, 0, unroll=True)


def plane_body(in_ref, f_ref, out_ref, wide_ref, bias_ref, bias_x_ref):
    rows = 4 * SIDE
    bias_x_ref[...] = same_line(rows, lambda i: i // SIDE)
    factors = (f_ref[0], f_ref[1])

    def step(b, _):
        parts = [in_ref[pl.ds(4 * b, 4), j].reshape(rows, LANES) for j in range(4)]
        for j, r in enumerate(attend([parts], factors, bias_x_ref[...])[0]):
            out_ref[j, pl.ds(4 * b, 4)] = r.reshape(4, 4, 8, LANES)
        return 0

    lax.fori_loop(0, 8, step, 0, unroll=4)

    def add(j, b, r):
        out_ref[j, :, b] += r

    strided_lines(in_ref, f_ref, wide_ref, bias_ref, add)


def depth_body(in_ref, f_ref, out_ref, flat_ref, res_ref, bias_ref):
    across = in_ref.shape[2]
    for j in range(4):
        flat_ref[j] = in_ref[:, j].astype(F32).reshape(SIDE * across, LANES)
    bias_ref[...] = same_line(4 * SIDE, lambda i: i // SIDE)
    factors = (f_ref[0], f_ref[1])
    spots = [[pl.ds(4 * b + i, SIDE, across) for i in range(4)] for b in range(across // 4)]
    blocks = [
        [jnp.concatenate([flat_ref[j, s] for s in four], axis=0).astype(BF) for j in range(4)]
        for four in spots
    ]
    for four, results in zip(spots, attend(blocks, factors, bias_ref[...])):
        for j, r in enumerate(results):
            for i, s in enumerate(four):
                res_ref[j, s] = r[i * SIDE : (i + 1) * SIDE]
    for j in range(4):
        out_ref[:, j] = res_ref[j].reshape(SIDE, across, LANES).astype(BF)


def halves(a):
    high = a.astype(BF)
    return high, (a - high.astype(F32)).astype(BF)


def combine_body(
    at_ref, loc_ref, back_ref, normed_ref, gain_ref, w_ref,
    away_ref, keep_ref, small_ref, g_ref, kept_ref, sum_ref,
):
    core = places(at_ref)[1]
    step = pl.program_id(0)
    rows = normed_ref.shape[0]
    kept_ref[...] = normed_ref[...]
    for j in range(4):
        part = loc_ref[j].reshape(rows, LANES) + back_ref[:, :, :, j].astype(F32).reshape(rows, LANES)
        at = (j - 1) % 4
        g_ref[:, at * LANES : (at + 1) * LANES] = part.astype(BF)

    @pl.when(step == 0)
    def _():
        sum_ref[...] = jnp.zeros_like(sum_ref)

    grads = g_ref[:, : 3 * LANES]
    total = jnp.zeros((rows, LANES), F32)
    for i in range(4):
        spots = [rows_at(2 * i + core, LANES), rows_at(2 * i + 1 - core, LANES)]
        w = jnp.concatenate([w_ref[s] for s in spots], axis=0)
        part = dot(grads, w, 1, 1).astype(BF)
        keep_ref[i] = part[:, :LANES]
        away_ref[i] = part[:, LANES:]
        n = jnp.concatenate([normed_ref[:, s] for s in spots], axis=1)
        both = part.astype(F32) * n.astype(F32)
        total += both[:, :LANES] + both[:, LANES:]
        sum_ref[i] += jnp.sum(both.reshape(rows // 8, 8, 2 * LANES), axis=0)
    for i in range(rows // LANES):
        row = jnp.sum(total[i * LANES : (i + 1) * LANES].T, axis=0, keepdims=True)
        small_ref[pl.ds(step * (rows // LANES) + i, 1)] = row

    @pl.when(step == pl.num_programs(0) - 1)
    def _():
        for i in range(8):
            h = 2 * (i % 4) + (1 - core if i < 4 else core)
            both = jnp.sum(sum_ref[i % 4], axis=0, keepdims=True)
            mine = both[:, LANES:] if i < 4 else both[:, :LANES]
            small_ref[8 + i : 9 + i] = mine / gain_ref[pl.ds(h, 1)]


def pair_body(at_ref, got_ref, keep_ref, small_ref, sgot_ref, *refs):
    sends, tinies, own_ref, both_ref, gown_ref, gain_buf = (
        refs[:3], refs[3:6], refs[6], refs[7], refs[8], refs[9]
    )
    zl = places(at_ref)[0]
    got = sgot_ref[...]
    dots = small_ref[:8] + got[:8]
    both_ref[...] = dots
    high, low = halves(dots)
    gain_buf[...] = jnp.concatenate([small_ref[12:16] + got[8:12]] * 2, axis=0)

    def block(i):
        return keep_ref[i].astype(F32) + got_ref[i].astype(F32)

    def gain(i):
        return jnp.broadcast_to(gain_buf[pl.ds(i, 1)], (8, LANES))

    for d, (ref, tiny) in enumerate(zip(sends, tinies)):
        to = (zl + d + 1) % 4
        ref[:TOK] = block(to).astype(BF)
        ref[TOK : TOK + 16] = jnp.concatenate([high, low], axis=0)
        tiny[...] = jnp.concatenate(halves(gain(to)), axis=0)
    own_ref[...] = block(zl)
    gown_ref[...] = gain(zl)


def tail_of(ref, at):
    return ref[at : at + 8].astype(F32) + ref[at + 8 : at + 16].astype(F32)


def weights_body(normed_ref, go_ref, g_ref, out_ref):
    three = dot(normed_ref[...], g_ref[:, : 3 * LANES], 0, 0)
    last = dot(go_ref[...], g_ref[:, 3 * LANES :], 0, 0)
    for j in range(4):
        part = three[:, j * LANES : (j + 1) * LANES] if j < 3 else last
        part = part.astype(BF).reshape(2, 2, 4, SIDE, LANES)
        for x in range(2):
            for zh in range(2):
                at = zh * LANES + j * SIDE
                out_ref[4 * x : 4 * x + 4, at : at + SIDE] = part[x, zh]


def tail_body(whole_ref, gown_ref, t1_ref, t2_ref, t3_ref, out_ref, buf, sem):
    del whole_ref
    gain = gown_ref[...]
    for ref in (t1_ref, t2_ref, t3_ref):
        gain = gain + tail_of(ref, 0)
    tail = jnp.concatenate(halves(gain), axis=0)
    buf[...] = jnp.broadcast_to(tail[None], (16, 16, LANES))
    copy = pltpu.make_async_copy(buf, out_ref.at[:, 2 * LANES :], sem)
    copy.start()
    copy.wait()


def sum_over(in_ref, at):
    acc = in_ref[0, at].astype(F32)
    for i in range(1, 16):
        acc = acc + in_ref[i, at].astype(F32)
    return acc


def plane_sum_body(at_ref, in_ref, send_ref, gain_ref):
    zh = places(at_ref)[3]
    gain = sum_over(in_ref, slice(2 * LANES, 2 * LANES + 16))
    gain = gain[:8] + gain[8:]
    gain_ref[...] = gain
    send_ref[:LANES] = sum_over(in_ref, rows_at(1 - zh, LANES)).astype(BF)
    send_ref[LANES:] = jnp.concatenate(halves(gain), axis=0)


def own_sum_body(at_ref, in_ref, own_ref):
    own_ref[...] = sum_over(in_ref, rows_at(places(at_ref)[3], LANES))


def last_body(own_ref, got_ref, gain_ref, q_ref, k_ref, v_ref, o_ref, gout_ref, *, scale):
    acc = (own_ref[...] + got_ref[:128].astype(F32)) * scale
    for j, ref in enumerate((q_ref, k_ref, v_ref)):
        ref[...] = acc[j * SIDE : (j + 1) * SIDE]
    o_ref[...] = acc[3 * SIDE :]
    gain = (gain_ref[...] + tail_of(got_ref, 128)) * scale
    gout_ref[...] = gain[:1]


def norm_body(at_ref, x_ref, gain_ref, own_ref, r1_ref, r2_ref, r3_ref, dots_ref, inv_ref, gx_ref):
    grad = own_ref[...]
    dots = dots_ref[...]
    for ref in (r1_ref, r2_ref, r3_ref):
        grad = grad + ref[:TOK].astype(F32)
        dots = dots + tail_of(ref, TOK)
    cols = [jnp.broadcast_to(dots[i : i + 1], (LANES, LANES)).T for i in range(8)]
    row_dot = jnp.concatenate(cols, axis=0)
    x = x_ref[...].astype(F32)
    inv = inv_ref[...]
    gx = inv * gain_ref[...] * grad - x * (inv * inv) * row_dot * (1.0 / 1024)
    gx_ref[...] = gx.astype(BF)


SMEM = pl.BlockSpec(memory_space=pltpu.SMEM)
VMEM = pl.BlockSpec(memory_space=pltpu.VMEM)


PLANES = [[x * 8 + zh * 4 + y for x in range(4) for y in range(4)] for zh in range(2)]
OVER_Z = [(s, s ^ 4) for s in range(SIDE)]


HALVES = [[x * 8 + zh * 4 + y for zh in range(2) for x in range(4) for y in range(4)]]


def over_slab(a):
    return lax.all_to_all(a, "slab", 0, 0, tiled=True, axis_index_groups=HALVES)


def in_plane(a):
    return lax.all_to_all(a, "slab", 0, 0, tiled=True, axis_index_groups=PLANES)


def body(
    inputs, norm_gain, query_weight, key_weight, value_weight, out_weight, logit_scale, grad_output
):
    rows, width = inputs.shape
    head_dim = 64
    at = jnp.stack([lax.axis_index("head"), lax.axis_index("slab")]).astype(jnp.int32)
    factors = logit_scale / math.sqrt(head_dim)
    blk = 256
    whole = lambda dims: pl.BlockSpec(dims, lambda i: (0,) * len(dims))
    by_rows = lambda dims: pl.BlockSpec(dims, lambda i: (i,) + (0,) * (len(dims) - 1))

    mine = call(
        pack_body,
        shape((SIDE, 4 * LANES), BF),
        in_specs=[pl.BlockSpec(memory_space=pltpu.HBM)] * 4,
        scratch_shapes=[pltpu.VMEM((4, SIDE, LANES), BF), pltpu.SemaphoreType.DMA((4,))],
    )(*(stay(w) for w in (query_weight, key_weight, value_weight, out_weight.T)))
    other = lax.ppermute(mine, "slab", OVER_Z)
    spread = call(
        pair_up_body, shape((16, 2 * SIDE, 4 * LANES), BF), in_specs=[SMEM, VMEM, VMEM]
    )(at, mine, other)
    early, normed, inv = call(
        norm_stats_body,
        (shape((rows, width), BF), far((rows, width), BF), far((rows, LANES), F32)),
        grid=(rows // blk,),
        in_specs=[by_rows((blk, width)), whole((1, width))],
        out_specs=(by_rows((blk, width)), by_rows((blk, width)), by_rows((blk, LANES))),
    )(inputs, norm_gain.reshape(1, width))
    pieces = in_plane(spread)

    wide = 2 * blk
    proj, weights = call(
        project_body,
        (far((2, 4, 4, 4, SIDE, LANES), BF), far((width, 4 * LANES), BF)),
        grid=(rows // wide,),
        in_specs=[
            by_rows((wide, width)),
            by_rows((wide, width)),
            whole((16, 2 * SIDE, 4 * LANES)),
        ],
        out_specs=(
            pl.BlockSpec((2, wide // 256, 4, 4, SIDE, LANES), lambda i: (0, i, 0, 0, 0, 0)),
            pl.BlockSpec(memory_space=pltpu.HBM),
        ),
        scratch_shapes=[pltpu.VMEM((width, 4 * LANES), BF), pltpu.SemaphoreType.DMA],
    )(early, grad_output, pieces)

    proj = proj.reshape(SIDE, 4, SIDE, LANES)
    z_in = over_slab(proj)
    big = (4, SIDE, 4, 8, LANES)
    local = call(
        plane_body,
        far(big, F32),
        in_specs=[VMEM, SMEM],
        scratch_shapes=[
            pltpu.VMEM(big, F32),
            pltpu.VMEM((256, 256), F32),
            pltpu.VMEM((128, 128), F32),
        ],
    )(stay(proj), factors)
    z_terms = call(
        depth_body,
        far((SIDE, 4, SIDE, LANES), BF),
        grid=(2,),
        in_specs=[pl.BlockSpec((SIDE, 4, 16, LANES), lambda i: (0, 0, i, 0)), SMEM],
        out_specs=pl.BlockSpec((SIDE, 4, 16, LANES), lambda i: (0, 0, i, 0)),
        scratch_shapes=[
            pltpu.VMEM((4, SIDE * 16, LANES), F32),
            pltpu.VMEM((4, SIDE * 16, LANES), F32),
            pltpu.VMEM((128, 128), F32),
        ],
    )(z_in, factors)
    back = over_slab(z_terms).reshape(2, 4, 4, 4, SIDE, LANES)
    local = local.reshape(4, 2, 4, 4, 4, 8, LANES)

    parts4 = pl.BlockSpec((4, blk, LANES), lambda i: (0, i, 0))
    away, keep, small, grads, early = call(
        combine_body,
        (
            shape((4, TOK, LANES), BF),
            shape((4, TOK, LANES), BF),
            shape((16, LANES), F32),
            shape((TOK, 4 * LANES), BF),
            shape((rows, width), BF),
        ),
        grid=(rows // blk,),
        in_specs=[
            SMEM,
            pl.BlockSpec((4, 2, 1, 4, 4, 8, LANES), lambda i: (0, 0, i, 0, 0, 0, 0)),
            pl.BlockSpec((2, 1, 4, 4, SIDE, LANES), lambda i: (0, i, 0, 0, 0, 0)),
            by_rows((blk, width)),
            whole((8, LANES)),
            whole((width, 3 * LANES)),
        ],
        out_specs=(
            parts4,
            parts4,
            whole((16, LANES)),
            by_rows((blk, 4 * LANES)),
            by_rows((blk, width)),
        ),
        scratch_shapes=[pltpu.VMEM((4, 8, 2 * LANES), F32)],
    )(at, stay(local), back, stay(normed), norm_gain.reshape(8, LANES), stay(weights))

    swap = [(i, i ^ 1) for i in range(8)]
    got = lax.ppermute(away, "head", swap)
    got_small = lax.ppermute(small, "head", swap)
    piece, tiny, row8 = (
        shape((TOK + 16, LANES), BF),
        shape((16, LANES), BF),
        shape((8, LANES), F32),
    )
    *sends, own, dots, gown = call(
        pair_body,
        (piece,) * 3 + (tiny,) * 3 + (shape((TOK, LANES), F32), row8, row8),
        in_specs=[SMEM] + [VMEM] * 4,
        scratch_shapes=[pltpu.VMEM((8, LANES), F32)],
    )(at, got, keep, small, got_small)
    to_zl = lambda d: [(i, (i + 2 * d) % 8) for i in range(8)]
    tinies = [lax.ppermute(s, "head", to_zl(d + 1)) for d, s in enumerate(sends[3:])]
    parts = []
    for d, s in enumerate(sends[:3]):
        parts.append(lax.ppermute(s, "head", to_zl(d + 1)))

    sent = call(
        weights_body,
        shape((16, 272, LANES), BF),
        grid=(2,),
        in_specs=[
            pl.BlockSpec((rows, 512), lambda i: (0, i)),
            pl.BlockSpec((rows, 512), lambda i: (0, i)),
            whole((rows, 4 * LANES)),
        ],
        out_specs=by_rows((8, 272, LANES)),
    )(early, grad_output, grads)
    anywhere = pl.BlockSpec(memory_space=pl.ANY)
    sent = call(
        tail_body,
        shape((16, 272, LANES), BF),
        in_specs=[anywhere] + [VMEM] * 4,
        out_specs=anywhere,
        scratch_shapes=[pltpu.VMEM((16, 16, LANES), BF), pltpu.SemaphoreType.DMA],
        input_output_aliases={0: 0},
    )(sent, gown, *tinies)
    pieces = in_plane(sent)
    send, gain = call(
        plane_sum_body, (shape((LANES + 16, LANES), BF), row8), in_specs=[SMEM, VMEM]
    )(at, pieces)
    other = lax.ppermute(send, "slab", OVER_Z)
    mine = call(
        own_sum_body, shape((LANES, LANES), F32), in_specs=[SMEM, VMEM]
    )(at, pieces)
    part = shape((SIDE, LANES), F32)
    gqw, gkw, gvw, gow, ggain = call(
        functools.partial(last_body, scale=1.0 / math.sqrt(rows * SIDE)),
        (part, part, part, part, shape((1, LANES), F32)),
    )(mine, other, gain)

    all_of = lambda dims: pl.BlockSpec(dims, lambda i, h: (0,) * len(dims))
    grad_inputs = pl.pallas_call(
        norm_body,
        out_shape=shape((rows, LANES), BF),
        name="norm_back",
        grid_spec=pltpu.PrefetchScalarGridSpec(
            num_scalar_prefetch=1,
            grid=(1,),
            in_specs=[
                pl.BlockSpec((rows, LANES), lambda i, h: (0, h[0])),
                pl.BlockSpec((1, LANES), lambda i, h: (0, h[0])),
                all_of((TOK, LANES)),
                all_of((TOK + 16, LANES)),
                all_of((TOK + 16, LANES)),
                all_of((TOK + 16, LANES)),
                all_of((8, LANES)),
                all_of((TOK, LANES)),
            ],
            out_specs=all_of((rows, LANES)),
        ),
        compiler_params=pltpu.CompilerParams(vmem_limit_bytes=VM),
    )(at, inputs, norm_gain.reshape(1, width), own, *parts, dots, inv)
    return grad_inputs, ggain.reshape(LANES), gqw, gkw, gvw, gow.T


def solution(mesh):
    in_specs = (
        P("slab", None),
        P(),
        P("slab", "head"),
        P("slab", "head"),
        P("slab", "head"),
        P("head", "slab"),
        P("head"),
        P("slab", None),
    )
    out_specs = (
        P("slab", "head"),
        P("head"),
        P("slab", "head"),
        P("slab", "head"),
        P("slab", "head"),
        P("head", "slab"),
    )

    return jax.shard_map(
        body, mesh=mesh, in_specs=in_specs, out_specs=out_specs, check_vma=False
    )
```

```python
import functools
import math

import jax
import jax.numpy as jnp
from jax import lax
from jax.experimental import pallas as pl
from jax.experimental.pallas import tpu as pltpu
from jax.sharding import PartitionSpec as P


BF = jnp.bfloat16
F32 = jnp.float32
SIDE = 32
LANES = 128
TOK = SIDE * SIDE
NEG = -1e30
VM = 20 << 20


def dot(a, b, ca, cb):
    return lax.dot_general(a, b, (((ca,), (cb,)), ((), ())), preferred_element_type=F32)


def call(body, outs, **kw):
    return pl.pallas_call(
        body,
        out_shape=outs,
        compiler_params=pltpu.CompilerParams(vmem_limit_bytes=VM),
        **kw,
    )


def shape(dims, kind):
    return jax.ShapeDtypeStruct(dims, kind)


def far(dims, kind):
    return pltpu.HBM(dims, kind)


def stay(a):
    return pltpu.with_memory_space_constraint(a, pltpu.HBM)


def places(at_ref):
    head, slab = at_ref[0], at_ref[1]
    return head // 2, head % 2, slab // 8, (slab // 4) % 2, slab % 4


def rows_at(i, count):
    return pl.ds(pl.multiple_of(i * count, count), count)


def pack_body(q_ref, k_ref, v_ref, o_ref, out_ref, buf, sems):
    copies = [
        pltpu.make_async_copy(src, buf.at[j], sems.at[j])
        for j, src in enumerate((q_ref, k_ref, v_ref, o_ref))
    ]
    for c in copies:
        c.start()
    for c in copies:
        c.wait()
    for j in range(4):
        out_ref[:, j * LANES : (j + 1) * LANES] = buf[j]


def pair_up_body(at_ref, mine_ref, got_ref, out_ref):
    _, _, _, zh, _ = places(at_ref)
    for place, ref in ((zh, mine_ref), (1 - zh, got_ref)):
        out_ref[:, rows_at(place, SIDE)] = jnp.broadcast_to(ref[...][None], (16, *ref.shape))


def norm_stats_body(x_ref, gain_ref, normed_ref, kept_ref, inv_ref):
    x = x_ref[...].astype(F32)
    width = x.shape[1]
    inv = lax.rsqrt(jnp.sum(x * x, axis=1, keepdims=True) / width + 1e-06)
    normed = (x * inv * gain_ref[...]).astype(BF)
    normed_ref[...] = normed
    kept_ref[...] = normed
    inv_ref[...] = jnp.broadcast_to(inv, inv_ref.shape)


def weights_of(pieces_ref, x):
    both = [pieces_ref[4 * x : 4 * x + 4, zh * SIDE : (zh + 1) * SIDE] for zh in range(2)]
    return jnp.concatenate([a.reshape(4 * SIDE, a.shape[-1]) for a in both], axis=0)


def project_body(normed_ref, go_ref, pieces_ref, out_ref, wout_ref, w_ref, sem):
    copy = pltpu.make_async_copy(w_ref, wout_ref, sem)

    @pl.when(pl.program_id(0) == 0)
    def _():
        for x in range(4):
            w_ref[256 * x : 256 * (x + 1)] = weights_of(pieces_ref, x)
        copy.start()

    rows = normed_ref.shape[0]
    three = dot(normed_ref[...], w_ref[:, : 3 * LANES], 1, 0)
    last = dot(go_ref[...], w_ref[:, 3 * LANES :], 1, 0)
    for j in range(4):
        part = three[:, j * LANES : (j + 1) * LANES] if j < 3 else last
        part = part.astype(BF).reshape(rows // 256, 2, 4, SIDE, LANES)
        for zh in range(2):
            out_ref[zh, :, :, j] = part[:, zh]

    @pl.when(pl.program_id(0) == pl.num_programs(0) - 1)
    def _():
        copy.wait()


def first_head(rows):
    return lax.broadcasted_iota(jnp.int32, (rows, LANES), 1) < LANES // 2


def stacked(a):
    rows = a.shape[0]
    keep = first_head(rows)
    zero = jnp.zeros_like(a)
    return jnp.concatenate([jnp.where(keep, a, zero), jnp.where(keep, zero, a)], axis=0)


def folded(a):
    rows = a.shape[0] // 2
    return jnp.where(first_head(rows), a[:rows], a[rows:])


def attend(blocks, factors, bias):
    rows = bias.shape[0]
    keep = first_head(rows)
    cut = [slice(0, rows), slice(rows, 2 * rows)]
    k2 = [stacked(k) for _, k, _, _ in blocks]
    v2 = [stacked(v) for _, _, v, _ in blocks]
    s = [dot(blk[0], k, 1, 1) for blk, k in zip(blocks, k2)]
    dp = [dot(blk[3], v, 1, 1) for blk, v in zip(blocks, v2)]
    s = [[m[:, c] * f + bias for c, f in zip(cut, factors)] for m in s]
    top = [[jnp.max(m, axis=1, keepdims=True) for m in pair] for pair in s]
    e = [[jnp.exp(m - t) for m, t in zip(*both)] for both in zip(s, top)]
    total = [[1.0 / jnp.sum(m, axis=1, keepdims=True) for m in pair] for pair in e]
    p = [[m * t for m, t in zip(*both)] for both in zip(e, total)]
    pb = [jnp.concatenate([m.astype(BF) for m in pair], axis=1) for pair in p]
    out = [dot(m, v, 1, 0) for m, v in zip(pb, v2)]
    go = [blk[3].astype(F32) * o for blk, o in zip(blocks, out)]
    delta = [
        [
            jnp.sum(jnp.where(keep, m, 0.0), axis=1, keepdims=True),
            jnp.sum(jnp.where(keep, 0.0, m), axis=1, keepdims=True),
        ]
        for m in go
    ]
    ds = [
        jnp.concatenate(
            [
                (ph * (d[:, c] - t) * f).astype(BF)
                for ph, t, c, f in zip(pair, deltas, cut, factors)
            ],
            axis=1,
        )
        for pair, d, deltas in zip(p, dp, delta)
    ]
    gv = [folded(dot(m, blk[3], 0, 0)) for m, blk in zip(pb, blocks)]
    gq = [dot(m, k, 1, 0) for m, k in zip(ds, k2)]
    gk = [folded(dot(m, blk[0], 0, 0)) for m, blk in zip(ds, blocks)]
    return list(zip(out, gq, gk, gv))


def same_line(rows, line):
    a = line(lax.broadcasted_iota(jnp.int32, (rows, rows), 0))
    b = line(lax.broadcasted_iota(jnp.int32, (rows, rows), 1))
    return jnp.where(a == b, 0.0, NEG).astype(F32)


def strided_lines(in_ref, f_ref, wide_ref, bias_ref, add):
    count = in_ref.shape[2] // 8
    for j in range(4):
        wide_ref[j] = in_ref[:, j].astype(F32).reshape(SIDE, count, 8, LANES)
    rows = 8 * SIDE
    bias_ref[...] = same_line(rows, lambda i: i % 8)
    factors = (f_ref[0], f_ref[1])

    def step(b, _):
        parts = [wide_ref[j, :, b].reshape(rows, LANES).astype(BF) for j in range(4)]
        for j, r in enumerate(attend([parts], factors, bias_ref[...])[0]):
            add(j, b, r.reshape(SIDE, 8, LANES))
        return 0

    lax.fori_loop(0, count, step, 0, unroll=True)


def plane_body(in_ref, f_ref, out_ref, wide_ref, bias_ref, bias_x_ref):
    rows = 4 * SIDE
    bias_x_ref[...] = same_line(rows, lambda i: i // SIDE)
    factors = (f_ref[0], f_ref[1])

    def step(b, _):
        parts = [in_ref[pl.ds(4 * b, 4), j].reshape(rows, LANES) for j in range(4)]
        for j, r in enumerate(attend([parts], factors, bias_x_ref[...])[0]):
            out_ref[j, pl.ds(4 * b, 4)] = r.reshape(4, 4, 8, LANES)
        return 0

    lax.fori_loop(0, 8, step, 0, unroll=4)

    def add(j, b, r):
        out_ref[j, :, b] += r

    strided_lines(in_ref, f_ref, wide_ref, bias_ref, add)


def depth_body(in_ref, f_ref, out_ref, flat_ref, res_ref, bias_ref):
    across = in_ref.shape[2]
    for j in range(4):
        flat_ref[j] = in_ref[:, j].astype(F32).reshape(SIDE * across, LANES)
    bias_ref[...] = same_line(4 * SIDE, lambda i: i // SIDE)
    factors = (f_ref[0], f_ref[1])
    spots = [[pl.ds(4 * b + i, SIDE, across) for i in range(4)] for b in range(across // 4)]
    blocks = [
        [jnp.concatenate([flat_ref[j, s] for s in four], axis=0).astype(BF) for j in range(4)]
        for four in spots
    ]
    for four, results in zip(spots, attend(blocks, factors, bias_ref[...])):
        for j, r in enumerate(results):
            for i, s in enumerate(four):
                res_ref[j, s] = r[i * SIDE : (i + 1) * SIDE]
    for j in range(4):
        out_ref[:, j] = res_ref[j].reshape(SIDE, across, LANES).astype(BF)


def halves(a):
    high = a.astype(BF)
    return high, (a - high.astype(F32)).astype(BF)


def combine_body(
    at_ref, loc_ref, back_ref, normed_ref, gain_ref, w_ref,
    away_ref, keep_ref, small_ref, g_ref, kept_ref, sum_ref,
):
    core = places(at_ref)[1]
    step = pl.program_id(0)
    rows = normed_ref.shape[0]
    kept_ref[...] = normed_ref[...]
    for j in range(4):
        part = jnp.concatenate(
            [
                loc_ref[j, :, x].reshape(256, LANES)
                + back_ref[:, x, :, j].astype(F32).reshape(256, LANES)
                for x in range(rows // 256)
            ],
            axis=0,
        )
        at = (j - 1) % 4
        g_ref[:, at * LANES : (at + 1) * LANES] = part.astype(BF)

    @pl.when(step == 0)
    def _():
        sum_ref[...] = jnp.zeros_like(sum_ref)

    grads = g_ref[:, : 3 * LANES]
    total = jnp.zeros((rows, LANES), F32)
    for i in range(4):
        spots = [rows_at(2 * i + core, LANES), rows_at(2 * i + 1 - core, LANES)]
        w = jnp.concatenate([w_ref[s] for s in spots], axis=0)
        part = dot(grads, w, 1, 1).astype(BF)
        keep_ref[i] = part[:, :LANES]
        away_ref[i] = part[:, LANES:]
        n = jnp.concatenate([normed_ref[:, s] for s in spots], axis=1)
        both = part.astype(F32) * n.astype(F32)
        total += both[:, :LANES] + both[:, LANES:]
        sum_ref[i] += jnp.sum(both.reshape(rows // 8, 8, 2 * LANES), axis=0)
    for i in range(rows // LANES):
        row = jnp.sum(total[i * LANES : (i + 1) * LANES].T, axis=0, keepdims=True)
        small_ref[pl.ds(step * (rows // LANES) + i, 1)] = row

    @pl.when(step == pl.num_programs(0) - 1)
    def _():
        for i in range(8):
            h = 2 * (i % 4) + (1 - core if i < 4 else core)
            both = jnp.sum(sum_ref[i % 4], axis=0, keepdims=True)
            mine = both[:, LANES:] if i < 4 else both[:, :LANES]
            small_ref[8 + i : 9 + i] = mine / gain_ref[pl.ds(h, 1)]


def pair_body(at_ref, got_ref, keep_ref, small_ref, sgot_ref, *refs):
    sends, tinies, own_ref, both_ref, gown_ref, gain_buf = (
        refs[:3], refs[3:6], refs[6], refs[7], refs[8], refs[9]
    )
    zl = places(at_ref)[0]
    got = sgot_ref[...]
    dots = small_ref[:8] + got[:8]
    both_ref[...] = dots
    high, low = halves(dots)
    gain_buf[...] = jnp.concatenate([small_ref[12:16] + got[8:12]] * 2, axis=0)

    def block(i):
        return keep_ref[i].astype(F32) + got_ref[i].astype(F32)

    def gain(i):
        return jnp.broadcast_to(gain_buf[pl.ds(i, 1)], (8, LANES))

    for d, (ref, tiny) in enumerate(zip(sends, tinies)):
        to = (zl + d + 1) % 4
        ref[:TOK] = block(to).astype(BF)
        ref[TOK : TOK + 16] = jnp.concatenate([high, low], axis=0)
        tiny[...] = jnp.concatenate(halves(gain(to)), axis=0)
    own_ref[...] = block(zl)
    gown_ref[...] = gain(zl)


def tail_of(ref, at):
    return ref[at : at + 8].astype(F32) + ref[at + 8 : at + 16].astype(F32)


def weights_body(normed_ref, go_ref, g_ref, out_ref):
    three = dot(normed_ref[...], g_ref[:, : 3 * LANES], 0, 0)
    last = dot(go_ref[...], g_ref[:, 3 * LANES :], 0, 0)
    for j in range(4):
        part = three[:, j * LANES : (j + 1) * LANES] if j < 3 else last
        part = part.astype(BF).reshape(2, 2, 4, SIDE, LANES)
        for x in range(2):
            for zh in range(2):
                at = zh * LANES + j * SIDE
                out_ref[4 * x : 4 * x + 4, at : at + SIDE] = part[x, zh]


def tail_body(whole_ref, gown_ref, t1_ref, t2_ref, t3_ref, out_ref, buf, sem):
    del whole_ref
    gain = gown_ref[...]
    for ref in (t1_ref, t2_ref, t3_ref):
        gain = gain + tail_of(ref, 0)
    tail = jnp.concatenate(halves(gain), axis=0)
    buf[...] = jnp.broadcast_to(tail[None], (16, 16, LANES))
    copy = pltpu.make_async_copy(buf, out_ref.at[:, 2 * LANES :], sem)
    copy.start()
    copy.wait()


def sum_over(in_ref, at):
    acc = in_ref[0, at].astype(F32)
    for i in range(1, 16):
        acc = acc + in_ref[i, at].astype(F32)
    return acc


def plane_sum_body(at_ref, in_ref, send_ref, gain_ref):
    zh = places(at_ref)[3]
    gain = sum_over(in_ref, slice(2 * LANES, 2 * LANES + 16))
    gain = gain[:8] + gain[8:]
    gain_ref[...] = gain
    send_ref[:LANES] = sum_over(in_ref, rows_at(1 - zh, LANES)).astype(BF)
    send_ref[LANES:] = jnp.concatenate(halves(gain), axis=0)


def own_sum_body(at_ref, in_ref, own_ref):
    own_ref[...] = sum_over(in_ref, rows_at(places(at_ref)[3], LANES))


def last_body(own_ref, got_ref, gain_ref, q_ref, k_ref, v_ref, o_ref, gout_ref, *, scale):
    acc = (own_ref[...] + got_ref[:128].astype(F32)) * scale
    for j, ref in enumerate((q_ref, k_ref, v_ref)):
        ref[...] = acc[j * SIDE : (j + 1) * SIDE]
    o_ref[...] = acc[3 * SIDE :]
    gain = (gain_ref[...] + tail_of(got_ref, 128)) * scale
    gout_ref[...] = gain[:1]


def norm_body(at_ref, x_ref, gain_ref, own_ref, r1_ref, r2_ref, r3_ref, dots_ref, inv_ref, gx_ref):
    grad = own_ref[...]
    dots = dots_ref[...]
    for ref in (r1_ref, r2_ref, r3_ref):
        grad = grad + ref[:TOK].astype(F32)
        dots = dots + tail_of(ref, TOK)
    cols = [jnp.broadcast_to(dots[i : i + 1], (LANES, LANES)).T for i in range(8)]
    row_dot = jnp.concatenate(cols, axis=0)
    x = x_ref[...].astype(F32)
    inv = inv_ref[...]
    gx = inv * gain_ref[...] * grad - x * (inv * inv) * row_dot * (1.0 / 1024)
    gx_ref[...] = gx.astype(BF)


SMEM = pl.BlockSpec(memory_space=pltpu.SMEM)
VMEM = pl.BlockSpec(memory_space=pltpu.VMEM)


PLANES = [[x * 8 + zh * 4 + y for x in range(4) for y in range(4)] for zh in range(2)]
OVER_Z = [(s, s ^ 4) for s in range(SIDE)]


HALVES = [[x * 8 + zh * 4 + y for zh in range(2) for x in range(4) for y in range(4)]]


def over_slab(a):
    return lax.all_to_all(a, "slab", 0, 0, tiled=True, axis_index_groups=HALVES)


def in_plane(a):
    return lax.all_to_all(a, "slab", 0, 0, tiled=True, axis_index_groups=PLANES)


def body(
    inputs, norm_gain, query_weight, key_weight, value_weight, out_weight, logit_scale, grad_output
):
    rows, width = inputs.shape
    head_dim = 64
    at = jnp.stack([lax.axis_index("head"), lax.axis_index("slab")]).astype(jnp.int32)
    factors = logit_scale / math.sqrt(head_dim)
    blk = 256
    whole = lambda dims: pl.BlockSpec(dims, lambda i: (0,) * len(dims))
    by_rows = lambda dims: pl.BlockSpec(dims, lambda i: (i,) + (0,) * (len(dims) - 1))

    mine = call(
        pack_body,
        shape((SIDE, 4 * LANES), BF),
        in_specs=[pl.BlockSpec(memory_space=pltpu.HBM)] * 4,
        scratch_shapes=[pltpu.VMEM((4, SIDE, LANES), BF), pltpu.SemaphoreType.DMA((4,))],
    )(*(stay(w) for w in (query_weight, key_weight, value_weight, out_weight.T)))
    other = lax.ppermute(mine, "slab", OVER_Z)
    spread = call(
        pair_up_body, shape((16, 2 * SIDE, 4 * LANES), BF), in_specs=[SMEM, VMEM, VMEM]
    )(at, mine, other)
    early, normed, inv = call(
        norm_stats_body,
        (shape((rows, width), BF), far((rows, width), BF), far((rows, LANES), F32)),
        grid=(rows // blk,),
        in_specs=[by_rows((blk, width)), whole((1, width))],
        out_specs=(by_rows((blk, width)), by_rows((blk, width)), by_rows((blk, LANES))),
    )(inputs, norm_gain.reshape(1, width))
    pieces = in_plane(spread)

    wide = 2 * blk
    proj, weights = call(
        project_body,
        (far((2, 4, 4, 4, SIDE, LANES), BF), far((width, 4 * LANES), BF)),
        grid=(rows // wide,),
        in_specs=[
            by_rows((wide, width)),
            by_rows((wide, width)),
            whole((16, 2 * SIDE, 4 * LANES)),
        ],
        out_specs=(
            pl.BlockSpec((2, wide // 256, 4, 4, SIDE, LANES), lambda i: (0, i, 0, 0, 0, 0)),
            pl.BlockSpec(memory_space=pltpu.HBM),
        ),
        scratch_shapes=[pltpu.VMEM((width, 4 * LANES), BF), pltpu.SemaphoreType.DMA],
    )(early, grad_output, pieces)

    proj = proj.reshape(SIDE, 4, SIDE, LANES)
    z_in = over_slab(proj)
    big = (4, SIDE, 4, 8, LANES)
    local = call(
        plane_body,
        far(big, F32),
        in_specs=[VMEM, SMEM],
        scratch_shapes=[
            pltpu.VMEM(big, F32),
            pltpu.VMEM((256, 256), F32),
            pltpu.VMEM((128, 128), F32),
        ],
    )(stay(proj), factors)
    z_terms = call(
        depth_body,
        far((SIDE, 4, SIDE, LANES), BF),
        grid=(2,),
        in_specs=[pl.BlockSpec((SIDE, 4, 16, LANES), lambda i: (0, 0, i, 0)), SMEM],
        out_specs=pl.BlockSpec((SIDE, 4, 16, LANES), lambda i: (0, 0, i, 0)),
        scratch_shapes=[
            pltpu.VMEM((4, SIDE * 16, LANES), F32),
            pltpu.VMEM((4, SIDE * 16, LANES), F32),
            pltpu.VMEM((128, 128), F32),
        ],
    )(z_in, factors)
    back = over_slab(z_terms).reshape(2, 4, 4, 4, SIDE, LANES)
    local = local.reshape(4, 2, 4, 4, 4, 8, LANES)

    parts4 = pl.BlockSpec((4, wide, LANES), lambda i: (0, i, 0))
    away, keep, small, grads, early = call(
        combine_body,
        (
            shape((4, TOK, LANES), BF),
            shape((4, TOK, LANES), BF),
            shape((16, LANES), F32),
            shape((TOK, 4 * LANES), BF),
            shape((rows, width), BF),
        ),
        grid=(rows // wide,),
        in_specs=[
            SMEM,
            pl.BlockSpec((4, 2, 2, 4, 4, 8, LANES), lambda i: (0, 0, i, 0, 0, 0, 0)),
            pl.BlockSpec((2, 2, 4, 4, SIDE, LANES), lambda i: (0, i, 0, 0, 0, 0)),
            by_rows((wide, width)),
            whole((8, LANES)),
            whole((width, 3 * LANES)),
        ],
        out_specs=(
            parts4,
            parts4,
            whole((16, LANES)),
            by_rows((wide, 4 * LANES)),
            by_rows((wide, width)),
        ),
        scratch_shapes=[pltpu.VMEM((4, 8, 2 * LANES), F32)],
    )(at, stay(local), back, stay(normed), norm_gain.reshape(8, LANES), stay(weights))

    swap = [(i, i ^ 1) for i in range(8)]
    got = lax.ppermute(away, "head", swap)
    got_small = lax.ppermute(small, "head", swap)
    piece, tiny, row8 = (
        shape((TOK + 16, LANES), BF),
        shape((16, LANES), BF),
        shape((8, LANES), F32),
    )
    *sends, own, dots, gown = call(
        pair_body,
        (piece,) * 3 + (tiny,) * 3 + (shape((TOK, LANES), F32), row8, row8),
        in_specs=[SMEM] + [VMEM] * 4,
        scratch_shapes=[pltpu.VMEM((8, LANES), F32)],
    )(at, got, keep, small, got_small)
    to_zl = lambda d: [(i, (i + 2 * d) % 8) for i in range(8)]
    tinies = [lax.ppermute(s, "head", to_zl(d + 1)) for d, s in enumerate(sends[3:])]
    parts = []
    for d, s in enumerate(sends[:3]):
        parts.append(lax.ppermute(s, "head", to_zl(d + 1)))

    sent = call(
        weights_body,
        shape((16, 272, LANES), BF),
        grid=(2,),
        in_specs=[
            pl.BlockSpec((rows, 512), lambda i: (0, i)),
            pl.BlockSpec((rows, 512), lambda i: (0, i)),
            whole((rows, 4 * LANES)),
        ],
        out_specs=by_rows((8, 272, LANES)),
    )(early, grad_output, grads)
    anywhere = pl.BlockSpec(memory_space=pl.ANY)
    sent = call(
        tail_body,
        shape((16, 272, LANES), BF),
        in_specs=[anywhere] + [VMEM] * 4,
        out_specs=anywhere,
        scratch_shapes=[pltpu.VMEM((16, 16, LANES), BF), pltpu.SemaphoreType.DMA],
        input_output_aliases={0: 0},
    )(sent, gown, *tinies)
    pieces = in_plane(sent)
    send, gain = call(
        plane_sum_body, (shape((LANES + 16, LANES), BF), row8), in_specs=[SMEM, VMEM]
    )(at, pieces)
    other = lax.ppermute(send, "slab", OVER_Z)
    mine = call(
        own_sum_body, shape((LANES, LANES), F32), in_specs=[SMEM, VMEM]
    )(at, pieces)
    part = shape((SIDE, LANES), F32)
    gqw, gkw, gvw, gow, ggain = call(
        functools.partial(last_body, scale=1.0 / math.sqrt(rows * SIDE)),
        (part, part, part, part, shape((1, LANES), F32)),
    )(mine, other, gain)

    all_of = lambda dims: pl.BlockSpec(dims, lambda i, h: (0,) * len(dims))
    grad_inputs = pl.pallas_call(
        norm_body,
        out_shape=shape((rows, LANES), BF),
        name="norm_back",
        grid_spec=pltpu.PrefetchScalarGridSpec(
            num_scalar_prefetch=1,
            grid=(1,),
            in_specs=[
                pl.BlockSpec((rows, LANES), lambda i, h: (0, h[0])),
                pl.BlockSpec((1, LANES), lambda i, h: (0, h[0])),
                all_of((TOK, LANES)),
                all_of((TOK + 16, LANES)),
                all_of((TOK + 16, LANES)),
                all_of((TOK + 16, LANES)),
                all_of((8, LANES)),
                all_of((TOK, LANES)),
            ],
            out_specs=all_of((rows, LANES)),
        ),
        compiler_params=pltpu.CompilerParams(vmem_limit_bytes=VM),
    )(at, inputs, norm_gain.reshape(1, width), own, *parts, dots, inv)
    return grad_inputs, ggain.reshape(LANES), gqw, gkw, gvw, gow.T


def solution(mesh):
    in_specs = (
        P("slab", None),
        P(),
        P("slab", "head"),
        P("slab", "head"),
        P("slab", "head"),
        P("head", "slab"),
        P("head"),
        P("slab", None),
    )
    out_specs = (
        P("slab", "head"),
        P("head"),
        P("slab", "head"),
        P("slab", "head"),
        P("slab", "head"),
        P("head", "slab"),
    )

    return jax.shard_map(
        body, mesh=mesh, in_specs=in_specs, out_specs=out_specs, check_vma=False
    )
```
